256 devices in a mesh: pair: 64 (over x_hi, z, y), sigma: 4 (over x_lo, core).
Axes of the slice: x: 4 (x_hi: 2, x_lo: 2; x = x_hi * 2 + x_lo), y: 4, z: 8, core: 2. Of those that a mesh axis runs over, the one named last changes fastest.
Arguments:
- pair_density_matrices: bfloat16 [131072, 1536], P('pair'), may hold values from -16 to 16
- energy_bins: int32 [131072, 2], P('pair'), may hold values from 0 to 63
- bin_weights: float32 [2, 64], replicated, may hold values from 0.05 to 1
- coulomb: float32 [1536], replicated, may hold values from 0.5 to 4
- state_matrices: bfloat16 [1536, 2048], P(None, 'sigma'), may hold values from -6 to 6
Outputs:
- screened_states: float32 [1536, 2, 2048], P('pair', None, 'sigma')
- sigma_diag: float32 [2, 2048], P(None, 'sigma')
The draws below stay inside these ranges and needn't reach their ends.
All inputs are finite; a program needn't handle non-finite values.
Results may differ from the reference program's by a relative error of at most 0.00035.
Values sent between devices are 32-bit elements; how exact they have to be, the bound alone decides.
No kernel may reach another device: no remote copies, remote signals or barrier semaphores. Data moves between devices by JAX's collectives and lax.ppermute only.
A program may use at most 64 MiB of HBM per device.

```python
import math
import jax
import jax.numpy as jnp
from jax import lax

NG = 1536
NS = 2048
NF = 2
NBIN = 64
PAIRS = 131072


def set_ends(values, key, least, top_value):
    index_at = [jax.random.randint(jax.random.fold_in(key, axis), (), 0, length) for axis, length in enumerate(values.shape)]
    main_axis = values.shape.index(max(values.shape))
    beside = index_at[:main_axis] + [(index_at[main_axis] + 1) % values.shape[main_axis]] + index_at[main_axis + 1:]
    return values.at[tuple(index_at)].set(least).at[tuple(beside)].set(top_value)


def with_spikes(values, stream_key, source, target, parts, factor):
    def block_of(position):
        return (jnp.arange(values.shape[position]) // (values.shape[position] // parts)).reshape((-1,) + (1,) * (values.ndim - 1 - position))

    one_side = jax.random.permutation(stream_key, parts)[block_of(target)]
    far = (block_of(target) + parts // 2) % parts
    return jnp.where((block_of(source) == one_side) | (block_of(source) == far), factor * values, values)


def block_levels(key, extent, pieces, least, high):
    level = 1.0
    for axis_at, parts in pieces:
        heights = jax.random.uniform(jax.random.fold_in(jax.random.fold_in(key, 6), axis_at), (parts,), jnp.float32, least / len(pieces), high / len(pieces))
        level = level * jnp.repeat(jnp.exp(heights), extent[axis_at] // parts).reshape((-1,) + (1,) * (len(extent) - 1 - axis_at))
    return level


def bell_draw(own_key, shape, scale, most, split=(), kind=jnp.bfloat16):
    entries = scale * jax.random.normal(own_key, shape, jnp.float32)
    if split:
        entries = entries * block_levels(own_key, shape, split, -0.22, 0.18)
    return jnp.clip(entries, -most, most).astype(kind)


def heavy_noise(key, dims, width, bound, pieces, heavy, kind=jnp.bfloat16):
    values = width * jax.random.normal(key, dims, jnp.float32)
    if pieces:
        values = values * block_levels(key, dims, pieces, -0.22, 0.18)
    return jnp.clip(with_spikes(values, jax.random.fold_in(key, 3), *heavy), -bound, bound).astype(kind)


def setup_inputs(seed: int = 0) -> dict:
    key_of = jax.random.split(jax.random.key(seed), 6)
    return {
        "pair_density_matrices": heavy_noise(key_of[0], (PAIRS, NG), 1.0, 16.0, ((0, 64),), (0, 1, 64, 4.0)),
        "energy_bins": set_ends(jax.random.randint(key_of[1], (PAIRS, NF), 0, NBIN), jax.random.fold_in(key_of[1], 1), 0, NBIN - 1).astype(jnp.int32),
        "bin_weights": jnp.clip(jnp.exp(jax.random.uniform(key_of[2], (NF, NBIN), jnp.float32, math.log(0.05), math.log(1.0))), 0.05, 1.0),
        "coulomb": jnp.clip(jnp.exp(jax.random.uniform(key_of[3], (NG,), jnp.float32, math.log(0.5), math.log(4.0))), 0.5, 4.0),
        "state_matrices": bell_draw(key_of[4], (NG, NS), 1.0, 6.0, ((1, 4),)),
    }


def reference(pair_density_matrices, energy_bins, bin_weights, coulomb, state_matrices):
    pair_total = pair_density_matrices.shape[0]
    freq_ids = jnp.arange(NF, dtype=jnp.int32)
    weight = bin_weights[freq_ids[None, :], energy_bins] / jnp.float32(pair_total)
    coulomb_root = jnp.sqrt(coulomb)
    pairs_wide = pair_density_matrices.astype(jnp.float32)
    states_wide = state_matrices.astype(jnp.float32)
    applied_list = []
    diagonal_entries_list = []
    for freq_index in range(NF):
        scaled_product = (weight[:, freq_index:freq_index + 1] * pairs_wide).astype(jnp.bfloat16)
        scaled_product = lax.optimization_barrier(scaled_product).astype(jnp.float32)
        polar = -jnp.dot(pairs_wide.T, scaled_product, precision=lax.Precision.HIGHEST)
        screened = coulomb_root[:, None] * polar * coulomb_root[None, :]
        applied = jnp.dot(screened, states_wide, precision=lax.Precision.HIGHEST)
        applied_list.append(applied)
        diagonal_entries_list.append(lax.optimization_barrier(jnp.sum(states_wide * applied, axis=0)) / jnp.float32(NG))
    screened_states = jnp.stack(applied_list, axis=1)
    sigma_diag = jnp.stack(diagonal_entries_list, axis=0)
    return (screened_states, sigma_diag)
```

```python
import jax
import jax.numpy as jnp
from jax import lax
from jax.sharding import PartitionSpec as P


NX, NZ, NY = 2, 8, 4
STREAMS = ((0, 256, "zy", (4, 3), (2, 1)), (256, 256, "yz", (3, 4), (2, 1)), (512, 256, "yz", (4, 3), (1, 2)))


def place(position):
    return position // (NZ * NY), position // NY % NZ, position % NY


def pair_perm(dx, dz, dy):
    moves = []
    for position in range(NX * NZ * NY):
        x, z, y = place(position)
        moves.append((position, ((x + dx) % NX * NZ + (z + dz) % NZ) * NY + (y + dy) % NY))
    return moves


def ring_sum(block, axis, me, size, hops, move):
    def own(target):
        return lax.dynamic_slice_in_dim(block, target % size, 1, axis)

    up, down = hops
    rising, falling = None, None
    for step in range(up):
        part = own(me + up - step)
        rising = lax.ppermute(part if rising is None else part + rising, "pair", move(1))
    for step in range(down):
        part = own(me - down + step)
        falling = lax.ppermute(part if falling is None else part + falling, "pair", move(-1))
    return own(me) + rising + falling


def local(pair_density_matrices, energy_bins, bin_weights, coulomb, state_matrices):
    pair_local, width = pair_density_matrices.shape
    pair_count = lax.axis_size("pair")
    sigma_count = lax.axis_size("sigma")
    row_count = width // pair_count
    col_count = width // sigma_count
    pair_position = lax.axis_index("pair")
    sigma_position = lax.axis_index("sigma")
    x, z, y = place(pair_position)
    quarter = sigma_position ^ (2 * x)

    bin_levels = jnp.arange(bin_weights.shape[1], dtype=jnp.int32)
    matches = (energy_bins[:, :, None] == bin_levels[None, None, :]).astype(jnp.float32)
    picked = jnp.sum(matches * bin_weights[None, :, :], axis=2)
    weight = picked / jnp.float32(pair_local * pair_count)
    slab = lax.dynamic_slice_in_dim(pair_density_matrices, quarter * col_count, col_count, 1).astype(jnp.float32)
    scaled = jnp.concatenate(
        [(weight[:, f : f + 1] * slab).astype(jnp.bfloat16) for f in range(weight.shape[1])], axis=1
    )
    sums = []
    for first, columns, order, z_hops, y_hops in STREAMS:
        part = lax.dot_general(
            pair_density_matrices,
            scaled[:, first : first + columns],
            (((0,), (0,)), ((), ())),
            preferred_element_type=jnp.float32,
        ).reshape(NX, NZ, NY, row_count, columns)
        for ring in order:
            if ring == "z":
                part = ring_sum(part, 1, z, NZ, z_hops, lambda d: pair_perm(0, d, 0))
            else:
                part = ring_sum(part, 2, y, NY, y_hops, lambda d: pair_perm(0, 0, d))
        sums.append(part.reshape(NX, row_count, columns))
    both = jnp.concatenate(sums, axis=2)
    swap = [
        (p * sigma_count + s, (p ^ (NZ * NY)) * sigma_count + (s ^ 2))
        for p in range(pair_count)
        for s in range(sigma_count)
    ]
    polar = lax.dynamic_index_in_dim(both, x, 0, False) + lax.ppermute(
        lax.dynamic_index_in_dim(both, 1 - x, 0, False), ("pair", "sigma"), swap
    )
    root = jnp.sqrt(coulomb)
    root_rows = lax.dynamic_slice_in_dim(root, pair_position * row_count, row_count, 0)
    root_columns = lax.dynamic_slice_in_dim(root, quarter * col_count, col_count, 0)
    screened = -root_rows[:, None, None] * polar.reshape(row_count, -1, col_count) * root_columns[None, None, :]
    parts = [screened] + [
        lax.ppermute(screened, "sigma", [(s, s ^ k) for s in range(sigma_count)]) for k in range(1, sigma_count)
    ]
    for bit in (1, 2):
        odd = (quarter & bit) != 0
        parts = [jnp.where(odd, parts[k ^ bit], parts[k]) for k in range(sigma_count)]
    states_wide = state_matrices.astype(jnp.float32)
    applied = jnp.einsum(
        "rfc,cn->rfn", jnp.concatenate(parts, axis=2), states_wide, precision=lax.Precision.HIGHEST
    )
    own_states = lax.dynamic_slice_in_dim(states_wide, pair_position * row_count, row_count, 0)
    total = jnp.sum(own_states[:, None, :] * applied, axis=0) / jnp.float32(width)
    for moves in (
        [(0, dz, 0) for dz in range(1, NZ)],
        [(dx, 0, dy) for dx in range(NX) for dy in range(NY) if dx or dy],
    ):
        total = sum([lax.ppermute(total, "pair", pair_perm(*m)) for m in moves], total)
    return (applied, total)


def solution(mesh):
    return jax.shard_map(
        local,
        mesh=mesh,
        in_specs=(P("pair", None), P("pair", None), P(), P(), P(None, "sigma")),
        out_specs=(P("pair", None, "sigma"), P(None, "sigma")),
        check_vma=False,
    )
```

```python
import jax
import jax.numpy as jnp
from jax import lax
from jax.experimental import pallas as pl
from jax.experimental.pallas import tpu as pltpu
from jax.sharding import PartitionSpec as P


NX, NZ, NY = 2, 8, 4
COLUMNS = 256
Y_GROUPS = [[base + y for y in range(NY)] for base in range(0, NX * NZ * NY, NY)]


def place(position):
    return position // (NZ * NY), position // NY % NZ, position % NY


def z_perm(dz):
    moves = []
    for position in range(NX * NZ * NY):
        x, z, y = place(position)
        moves.append((position, (x * NZ + (z + dz) % NZ) * NY + y))
    return moves


def x_swap(block):
    x = lax.axis_index("pair") // (NZ * NY)
    pair_count, sigma_count = lax.axis_size("pair"), lax.axis_size("sigma")
    moves = [
        (p * sigma_count + s, (p ^ (NZ * NY)) * sigma_count + (s ^ 2))
        for p in range(pair_count)
        for s in range(sigma_count)
    ]
    away = lax.dynamic_index_in_dim(block, 1 - x, 0, False)
    return lax.dynamic_index_in_dim(block, x, 0, False) + lax.ppermute(away, ("pair", "sigma"), moves)


def y_sum(block):
    return jnp.sum(lax.all_to_all(block, "pair", 0, 0, axis_index_groups=Y_GROUPS, tiled=True), axis=0)


def z_sum(block):
    z = lax.axis_index("pair") // NY % NZ
    half = block.shape[-1] // 2

    def own(*offsets):
        return jnp.stack([lax.dynamic_index_in_dim(block, (z + d) % NZ, 0, False) for d in offsets])

    def send(part, dz):
        return lax.ppermute(part, "pair", z_perm(dz))

    far, ahead, behind = lax.optimization_barrier((own(4)[0], own(1, 3), own(-1, -3)))
    low = send(far[..., :half], -2)
    high = send(far[..., half:], 2)
    up = send(ahead, 1)
    down = send(behind, -1)
    above, below = own(2, -2)
    above = above + up[1]
    below = below + down[1]
    above = jnp.concatenate([above[..., :half], above[..., half:] + high], axis=-1)
    below = jnp.concatenate([below[..., :half] + low, below[..., half:]], axis=-1)
    return own(0)[0] + up[0] + down[0] + send(above, 2) + send(below, -2)


def chi_columns(pairs, quarter, weight, first, blocks, block, where):
    pair_local, width = pairs.shape
    col_count = width // 4
    step_rows = 384

    def body(quarter_ref, pair_ref, slab_ref, weight_ref, out_ref, scaled_ref):
        @pl.when(pl.program_id(0) == 0)
        def _():
            by_pair = jnp.transpose(weight_ref[...])
            for t in range(COLUMNS // 128):
                f, column = divmod(first + 128 * t, col_count)
                product = by_pair[:, f : f + 1] * slab_ref[:, column : column + 128].astype(jnp.float32)
                scaled_ref[:, 128 * t : 128 * t + 128] = product.astype(jnp.bfloat16)

        result = lax.dot_general(
            pair_ref[...], scaled_ref[...], (((0,), (0,)), ((), ())), preferred_element_type=jnp.float32
        )
        for zz in range(4):
            for yy in range(NY):
                at = (zz * NY + yy) * 24
                out_ref[where(zz, yy)] = result[at : at + 24]

    return pl.pallas_call(
        body,
        grid_spec=pltpu.PrefetchScalarGridSpec(
            num_scalar_prefetch=1,
            grid=(width // step_rows,),
            in_specs=[
                pl.BlockSpec((pair_local, step_rows), lambda i, q: (0, i)),
                pl.BlockSpec((pair_local, col_count), lambda i, q: (0, q[0])),
                pl.BlockSpec(weight.shape, lambda i, q: (0, 0)),
            ],
            out_specs=pl.BlockSpec(block, lambda i, q: blocks[1](i)),
            scratch_shapes=[pltpu.VMEM((pair_local, COLUMNS), jnp.bfloat16)],
        ),
        out_shape=jax.ShapeDtypeStruct(blocks[0], jnp.float32),
    )(quarter, pairs, pairs, weight)


def local(pair_density_matrices, energy_bins, bin_weights, coulomb, state_matrices):
    pair_local, width = pair_density_matrices.shape
    pair_count = lax.axis_size("pair")
    sigma_count = lax.axis_size("sigma")
    row_count = width // pair_count
    col_count = width // sigma_count
    pair_position = lax.axis_index("pair")
    sigma_position = lax.axis_index("sigma")
    x = pair_position // (NZ * NY)
    quarter = sigma_position ^ (2 * x)

    bins = energy_bins.T
    bin_levels = jnp.arange(bin_weights.shape[1], dtype=jnp.int32)
    matches = (bins[:, None, :] == bin_levels[None, :, None]).astype(jnp.float32)
    weight = jnp.sum(matches * bin_weights[:, :, None], axis=1) / jnp.float32(pair_local * pair_count)
    weight = jnp.concatenate([weight, jnp.zeros((6, pair_local), jnp.float32)], axis=0)

    def columns(first, blocks, block, where):
        return chi_columns(
            pair_density_matrices, quarter.astype(jnp.int32)[None], weight, first, blocks, block, where
        )

    rc, n = row_count, COLUMNS
    b = columns(
        0, ((NY, NX, NZ, rc, n), lambda i: (0, i // 2, i % 2, 0, 0)), (NY, 1, 4, rc, n), lambda zz, yy: (yy, 0, zz)
    )
    c = columns(
        n, ((NX, NY, NZ, rc, n), lambda i: (i // 2, 0, i % 2, 0, 0)), (1, NY, 4, rc, n), lambda zz, yy: (0, yy, zz)
    )
    a = columns(
        2 * n, ((NZ, NY, NX, rc, n), lambda i: (i % 2, 0, i // 2, 0, 0)), (4, NY, 1, rc, n), lambda zz, yy: (zz, yy, 0)
    )
    b = x_swap(y_sum(b))
    c = y_sum(x_swap(c))
    bc = z_sum(jnp.concatenate([b, c], axis=2))
    a = x_swap(y_sum(z_sum(a)))
    polar = jnp.concatenate([bc, a], axis=1)

    root = jnp.sqrt(coulomb)
    root_rows = lax.dynamic_slice_in_dim(root, pair_position * row_count, row_count, 0)
    root_columns = lax.dynamic_slice_in_dim(root, quarter * col_count, col_count, 0)
    screened = -root_rows[:, None, None] * polar.reshape(row_count, -1, col_count) * root_columns[None, None, :]
    parts = [screened] + [
        lax.ppermute(screened, "sigma", [(s, s ^ k) for s in range(sigma_count)]) for k in range(1, sigma_count)
    ]
    for bit in (1, 2):
        odd = (quarter & bit) != 0
        parts = [jnp.where(odd, parts[k ^ bit], parts[k]) for k in range(sigma_count)]
    states_wide = state_matrices.astype(jnp.float32)
    applied = jnp.einsum(
        "rfc,cn->rfn", jnp.concatenate(parts, axis=2), states_wide, precision=lax.Precision.HIGHEST
    )
    own_states = lax.dynamic_slice_in_dim(states_wide, pair_position * row_count, row_count, 0)
    total = jnp.sum(own_states[:, None, :] * applied, axis=0) / jnp.float32(width)
    spread = jnp.broadcast_to(total.reshape(8, -1)[None], (pair_count, 8, total.size // 8))
    total = jnp.sum(lax.all_to_all(spread, "pair", 0, 0, tiled=True), axis=0).reshape(total.shape)
    return (applied, total)


def solution(mesh):
    return jax.shard_map(
        local,
        mesh=mesh,
        in_specs=(P("pair", None), P("pair", None), P(), P(), P(None, "sigma")),
        out_specs=(P("pair", None, "sigma"), P(None, "sigma")),
        check_vma=False,
    )
```

```python
import jax
import jax.numpy as jnp
from jax import lax
from jax.experimental import pallas as pl
from jax.experimental.pallas import tpu as pltpu
from jax.sharding import PartitionSpec as P


NX, NZ, NY = 2, 8, 4
COLUMNS = 256
STEP = 384
Z_ORDER = (4, 1, 3, -1, -3, 0, 2, -2)
Y_GROUPS = [[base + y for y in range(NY)] for base in range(0, NX * NZ * NY, NY)]


def place(position):
    return position // (NZ * NY), position // NY % NZ, position % NY


def z_perm(dz):
    moves = []
    for position in range(NX * NZ * NY):
        x, z, y = place(position)
        moves.append((position, (x * NZ + (z + dz) % NZ) * NY + y))
    return moves


def x_swap(away, keep):
    pair_count, sigma_count = lax.axis_size("pair"), lax.axis_size("sigma")
    moves = [
        (p * sigma_count + s, (p ^ (NZ * NY)) * sigma_count + (s ^ 2))
        for p in range(pair_count)
        for s in range(sigma_count)
    ]
    return keep + lax.ppermute(away, ("pair", "sigma"), moves)


def y_sum(block):
    return jnp.sum(lax.all_to_all(block, "pair", 0, 0, axis_index_groups=Y_GROUPS, tiled=True), axis=0)


def z_sum(low, high, up, down, keep):
    half = low.shape[-1]

    def send(part, dz):
        return lax.ppermute(part, "pair", z_perm(dz))

    low, high = send(low, -2), send(high, 2)
    up, down = send(up, 1), send(down, -1)
    above, below = keep[1] + up[1], keep[2] + down[1]
    above = jnp.concatenate([above[..., :half], above[..., half:] + high], axis=-1)
    below = jnp.concatenate([below[..., :half] + low, below[..., half:]], axis=-1)
    return keep[0] + up[0] + down[0] + send(above, 2) + send(below, -2)


def chi_columns(pairs, spot, weight, first, shapes, stores):
    pair_local, width = pairs.shape
    col_count = width // 4
    row_count = width // (NX * NZ * NY)
    steps = width // STEP

    def body(spot_ref, pair_ref, slab_ref, weight_ref, *refs):
        outs, scaled_ref, rows_ref = refs[: len(shapes)], refs[-2], refs[-1]
        step = pl.program_id(0)

        @pl.when(step == 0)
        def _():
            for t in range(COLUMNS // 128):
                f, column = divmod(first + 128 * t, col_count)
                turned = jnp.transpose(slab_ref[:, column : column + 128]).astype(jnp.float32)
                scaled_ref[128 * t : 128 * t + 128, :] = (weight_ref[f : f + 1, :] * turned).astype(jnp.bfloat16)

        result = jnp.dot(scaled_ref[...], pair_ref[...], preferred_element_type=jnp.float32)
        rows_ref[pl.ds(pl.multiple_of(step * STEP, STEP), STEP), :] = jnp.transpose(result)

        @pl.when(step == steps - 1)
        def _():
            x, z = spot_ref[1], spot_ref[2]
            for out, index, columns, keeps, dz, y in stores:
                at = ((x if keeps else 1 - x) * NZ + ((z + dz) & (NZ - 1))) * NY + y
                outs[out][index] = rows_ref[pl.ds(pl.multiple_of(at * row_count, 8), row_count), columns]

    whole = lambda shape: pl.BlockSpec(shape, lambda i, spot: (0,) * len(shape))
    return pl.pallas_call(
        body,
        grid_spec=pltpu.PrefetchScalarGridSpec(
            num_scalar_prefetch=1,
            grid=(steps,),
            in_specs=[
                pl.BlockSpec((pair_local, STEP), lambda i, spot: (0, i)),
                pl.BlockSpec((pair_local, col_count), lambda i, spot: (0, spot[0])),
                whole(weight.shape),
            ],
            out_specs=[whole(shape) for shape in shapes],
            scratch_shapes=[
                pltpu.VMEM((COLUMNS, pair_local), jnp.bfloat16),
                pltpu.VMEM((width, COLUMNS), jnp.float32),
            ],
        ),
        out_shape=[jax.ShapeDtypeStruct(shape, jnp.float32) for shape in shapes],
    )(spot, pairs, pairs, weight)


def local(pair_density_matrices, energy_bins, bin_weights, coulomb, state_matrices):
    pair_local, width = pair_density_matrices.shape
    pair_count = lax.axis_size("pair")
    sigma_count = lax.axis_size("sigma")
    row_count = width // pair_count
    col_count = width // sigma_count
    pair_position = lax.axis_index("pair")
    sigma_position = lax.axis_index("sigma")
    x = pair_position // (NZ * NY)
    quarter = sigma_position ^ (2 * x)

    bins = energy_bins.T
    bin_levels = jnp.arange(bin_weights.shape[1], dtype=jnp.int32)
    matches = (bins[:, None, :] == bin_levels[None, :, None]).astype(jnp.float32)
    weight = jnp.sum(matches * bin_weights[:, :, None], axis=1) / jnp.float32(pair_local * pair_count)
    spot = jnp.stack([quarter, x, pair_position // NY % NZ]).astype(jnp.int32)

    def columns(first, shapes, stores):
        return chi_columns(pair_density_matrices, spot, weight, first, shapes, stores)

    rc, n, half = row_count, COLUMNS, COLUMNS // 2
    every = slice(None)
    spots = [(y, keeps, k) for y in range(NY) for keeps in (0, 1) for k in range(NZ)]
    c = columns(n, [(NY, NZ, rc, n)] * 2, [(keeps, (y, k), every, keeps, Z_ORDER[k], y) for y, keeps, k in spots])
    b = columns(0, [(NY, NX, NZ, rc, n)], [(0, (y, keeps, k), every, keeps, Z_ORDER[k], y) for y, keeps, k in spots])[0]
    stores = []
    for y, keeps, k in spots:
        if Z_ORDER[k] == 4:
            stores += [(0, (y, keeps), slice(0, half), keeps, 4, y), (1, (y, keeps), slice(half, n), keeps, 4, y)]
        else:
            out, slot = divmod(k - 1, 2) if k < 5 else (2, k - 5)
            stores.append((2 + out, (slot, y, keeps), every, keeps, Z_ORDER[k], y))
    a = columns(2 * n, [(NY, NX, rc, half)] * 2 + [(k, NY, NX, rc, n) for k in (2, 2, 3)], stores)

    c = y_sum(x_swap(*c))
    b = x_swap(*y_sum(b))
    bc = jnp.concatenate([b, c], axis=2)
    bc = lax.optimization_barrier((bc[0, :, :n], bc[0, :, n:], bc[1:3], bc[3:5], bc[5:]))
    bc = z_sum(*bc)
    a = x_swap(*y_sum(z_sum(*a)))
    polar = jnp.concatenate([bc, a], axis=1)

    root = jnp.sqrt(coulomb)
    root_rows = lax.dynamic_slice_in_dim(root, pair_position * row_count, row_count, 0)
    root_columns = lax.dynamic_slice_in_dim(root, quarter * col_count, col_count, 0)
    screened = -root_rows[:, None, None] * polar.reshape(row_count, -1, col_count) * root_columns[None, None, :]
    parts = [screened] + [
        lax.ppermute(screened, "sigma", [(s, s ^ k) for s in range(sigma_count)]) for k in range(1, sigma_count)
    ]
    for bit in (1, 2):
        odd = (quarter & bit) != 0
        parts = [jnp.where(odd, parts[k ^ bit], parts[k]) for k in range(sigma_count)]
    states_wide = state_matrices.astype(jnp.float32)
    applied = jnp.einsum(
        "rfc,cn->rfn", jnp.concatenate(parts, axis=2), states_wide, precision=lax.Precision.HIGHEST
    )
    own_states = lax.dynamic_slice_in_dim(states_wide, pair_position * row_count, row_count, 0)
    total = jnp.sum(own_states[:, None, :] * applied, axis=0) / jnp.float32(width)
    spread = jnp.broadcast_to(total.reshape(8, -1)[None], (pair_count, 8, total.size // 8))
    total = jnp.sum(lax.all_to_all(spread, "pair", 0, 0, tiled=True), axis=0).reshape(total.shape)
    return (applied, total)


def solution(mesh):
    return jax.shard_map(
        local,
        mesh=mesh,
        in_specs=(P("pair", None), P("pair", None), P(), P(), P(None, "sigma")),
        out_specs=(P("pair", None, "sigma"), P(None, "sigma")),
        check_vma=False,
    )
```

```python
import jax
import jax.numpy as jnp
from jax import lax
from jax.experimental import pallas as pl
from jax.experimental.pallas import tpu as pltpu
from jax.sharding import PartitionSpec as P


NX, NZ, NY = 2, 8, 4
COLUMNS = 256
QUARTERS = 4
Z_ORDER = (4, 1, 3, -1, -3, 0, 2, -2)
Y_GROUPS = [[base + y for y in range(NY)] for base in range(0, NX * NZ * NY, NY)]


def place(position):
    return position // (NZ * NY), position // NY % NZ, position % NY


def z_perm(dz):
    moves = []
    for position in range(NX * NZ * NY):
        x, z, y = place(position)
        moves.append((position, (x * NZ + (z + dz) % NZ) * NY + y))
    return moves


def x_swap(away, keep):
    pair_count, sigma_count = lax.axis_size("pair"), lax.axis_size("sigma")
    moves = [
        (p * sigma_count + s, (p ^ (NZ * NY)) * sigma_count + (s ^ 2))
        for p in range(pair_count)
        for s in range(sigma_count)
    ]
    return keep + lax.ppermute(away, ("pair", "sigma"), moves)


def y_sum(block):
    return jnp.sum(lax.all_to_all(block, "pair", 0, 0, axis_index_groups=Y_GROUPS, tiled=True), axis=0)


def z_sum(low, high, up, down, keep):
    half = low.shape[-1]

    def send(part, dz):
        return lax.ppermute(part, "pair", z_perm(dz))

    low, high = send(low, -2), send(high, 2)
    up, down = send(up, 1), send(down, -1)
    above, below = keep[1] + up[1], keep[2] + down[1]
    above = jnp.concatenate([above[..., :half], above[..., half:] + high], axis=-1)
    below = jnp.concatenate([below[..., :half] + low, below[..., half:]], axis=-1)
    return keep[0] + up[0] + down[0] + send(above, 2) + send(below, -2)


def spots():
    position = lax.axis_index("pair")
    x = position // (NZ * NY)
    return lax.axis_index("sigma") ^ (2 * x), x, (position // NY) & (NZ - 1)


def chi_streams(pairs, bins, table, streams):
    pair_local, width = pairs.shape
    col_count = width // QUARTERS
    row_count = width // (NX * NZ * NY)
    total = COLUMNS * len(streams)
    shapes = [shape for stream, _ in streams for shape in stream]

    def body(pairs_ref, bins_ref, table_ref, *refs):
        pair_ref, scaled_ref, rows_ref, done = refs[len(shapes) :]
        quarter, x, z = spots()

        def first_column(step):
            return pl.multiple_of(((quarter + step) & (QUARTERS - 1)) * col_count, 128)

        def fetch(step):
            part = pairs_ref.at[:, pl.ds(first_column(step), col_count)]
            return pltpu.make_async_copy(part, pair_ref.at[step], done.at[step])

        for step in range(QUARTERS):
            fetch(step).start()
        index = bins_ref[...]
        upper = lax.broadcasted_iota(jnp.int32, index.shape, 0) > 0
        picked = jnp.zeros(index.shape, jnp.float32)
        for level in range(table.shape[1]):
            picked = jnp.where(index == level, jnp.where(upper, table_ref[1, level], table_ref[0, level]), picked)
        weight = picked / jnp.float32(pair_local * NX * NZ * NY)
        by_pair = jnp.transpose(jnp.concatenate([weight, jnp.zeros((6, pair_local), jnp.float32)], axis=0))
        fetch(0).wait()
        for t in range(total // 128):
            f, column = divmod(128 * t, col_count)
            product = by_pair[:, f : f + 1] * pair_ref[0, :, column : column + 128].astype(jnp.float32)
            scaled_ref[:, 128 * t : 128 * t + 128] = product.astype(jnp.bfloat16)
        for step in range(QUARTERS):
            if step:
                fetch(step).wait()
            rows_ref[pl.ds(first_column(step), col_count), :] = lax.dot_general(
                pair_ref[step], scaled_ref[...], (((0,), (0,)), ((), ())), preferred_element_type=jnp.float32
            )
        before = 0
        for k, (stream, stores) in enumerate(streams):
            for out, index, (left, right), keeps, dz, y in stores:
                at = ((x if keeps else 1 - x) * NZ + ((z + dz) & (NZ - 1))) * NY + y
                rows = pl.ds(pl.multiple_of(at * row_count, 8), row_count)
                refs[before + out][index] = rows_ref[rows, k * COLUMNS + left : k * COLUMNS + right]
            before += len(stream)

    outs = pl.pallas_call(
        body,
        in_specs=[
            pl.BlockSpec(memory_space=pltpu.HBM),
            pl.BlockSpec(memory_space=pltpu.VMEM),
            pl.BlockSpec(memory_space=pltpu.SMEM),
        ],
        out_specs=[pl.BlockSpec(memory_space=pltpu.VMEM)] * len(shapes),
        out_shape=[jax.ShapeDtypeStruct(shape, jnp.float32) for shape in shapes],
        scratch_shapes=[
            pltpu.VMEM((QUARTERS, pair_local, col_count), jnp.bfloat16),
            pltpu.VMEM((pair_local, total), jnp.bfloat16),
            pltpu.VMEM((width, total), jnp.float32),
            pltpu.SemaphoreType.DMA((QUARTERS,)),
        ],
        compiler_params=pltpu.CompilerParams(vmem_limit_bytes=36 << 20),
    )(pltpu.with_memory_space_constraint(pairs, pltpu.HBM), bins, table)
    split = []
    for stream, _ in streams:
        split.append(outs[: len(stream)])
        outs = outs[len(stream) :]
    return split


def local(pair_density_matrices, energy_bins, bin_weights, coulomb, state_matrices):
    width = pair_density_matrices.shape[1]
    pair_count = lax.axis_size("pair")
    sigma_count = lax.axis_size("sigma")
    row_count = width // pair_count
    col_count = width // sigma_count
    pair_position = lax.axis_index("pair")
    quarter = spots()[0]
    rc, n, half = row_count, COLUMNS, COLUMNS // 2
    every = (0, n)
    slots = [(y, keeps, k) for y in range(NY) for keeps in (0, 1) for k in range(NZ)]
    b_stores = [(0, (y, keeps, k), every, keeps, Z_ORDER[k], y) for y, keeps, k in slots]
    c_stores = [(keeps, (y, k), every, keeps, Z_ORDER[k], y) for y, keeps, k in slots]
    a_stores = []
    for y, keeps, k in slots:
        if Z_ORDER[k] == 4:
            a_stores += [(0, (y, keeps), (0, half), keeps, 4, y), (1, (y, keeps), (half, n), keeps, 4, y)]
        else:
            out, slot = divmod(k - 1, 2) if k < 5 else (2, k - 5)
            a_stores.append((2 + out, (slot, y, keeps), every, keeps, Z_ORDER[k], y))
    (b,), c, a = chi_streams(
        pair_density_matrices,
        energy_bins.T,
        bin_weights,
        [
            ([(NY, NX, NZ, rc, n)], b_stores),
            ([(NY, NZ, rc, n)] * 2, c_stores),
            ([(NY, NX, rc, half)] * 2 + [(k, NY, NX, rc, n) for k in (2, 2, 3)], a_stores),
        ],
    )

    c = y_sum(x_swap(*c))
    b = x_swap(*y_sum(b))
    bc = jnp.concatenate([b, c], axis=2)
    bc = lax.optimization_barrier((bc[0, :, :n], bc[0, :, n:], bc[1:3], bc[3:5], bc[5:]))
    bc = z_sum(*bc)
    a = x_swap(*y_sum(z_sum(*a)))
    polar = jnp.concatenate([bc, a], axis=1)

    root = jnp.sqrt(coulomb)
    root_rows = lax.dynamic_slice_in_dim(root, pair_position * row_count, row_count, 0)
    root_columns = lax.dynamic_slice_in_dim(root, quarter * col_count, col_count, 0)
    screened = -root_rows[:, None, None] * polar.reshape(row_count, -1, col_count) * root_columns[None, None, :]
    parts = [screened] + [
        lax.ppermute(screened, "sigma", [(s, s ^ k) for s in range(sigma_count)]) for k in range(1, sigma_count)
    ]
    for bit in (1, 2):
        odd = (quarter & bit) != 0
        parts = [jnp.where(odd, parts[k ^ bit], parts[k]) for k in range(sigma_count)]
    states_wide = state_matrices.astype(jnp.float32)
    applied = jnp.einsum(
        "rfc,cn->rfn", jnp.concatenate(parts, axis=2), states_wide, precision=lax.Precision.HIGHEST
    )
    own_states = lax.dynamic_slice_in_dim(states_wide, pair_position * row_count, row_count, 0)
    total = jnp.sum(own_states[:, None, :] * applied, axis=0) / jnp.float32(width)
    spread = jnp.broadcast_to(total.reshape(8, -1)[None], (pair_count, 8, total.size // 8))
    total = jnp.sum(lax.all_to_all(spread, "pair", 0, 0, tiled=True), axis=0).reshape(total.shape)
    return (applied, total)


def solution(mesh):
    return jax.shard_map(
        local,
        mesh=mesh,
        in_specs=(P("pair", None), P("pair", None), P(), P(), P(None, "sigma")),
        out_specs=(P("pair", None, "sigma"), P(None, "sigma")),
        check_vma=False,
    )
```

```python
import jax
import jax.numpy as jnp
from jax import lax
from jax.experimental import pallas as pl
from jax.experimental.pallas import tpu as pltpu
from jax.sharding import PartitionSpec as P


NX, NZ, NY = 2, 8, 4
COLUMNS = 256
QUARTERS = 4
Z_ORDER = (4, 1, 3, -1, -3, 0, 2, -2)
Z_SLICES = ((0, 1), (1, 3), (3, 5), (5, 6), (6, 7), (7, 8))
Y_GROUPS = [[base + y for y in range(NY)] for base in range(0, NX * NZ * NY, NY)]


def place(position):
    return position // (NZ * NY), position // NY % NZ, position % NY


def z_perm(dz):
    moves = []
    for position in range(NX * NZ * NY):
        x, z, y = place(position)
        moves.append((position, (x * NZ + (z + dz) % NZ) * NY + y))
    return moves


def x_swap(away, keep):
    pair_count, sigma_count = lax.axis_size("pair"), lax.axis_size("sigma")
    moves = [
        (p * sigma_count + s, (p ^ (NZ * NY)) * sigma_count + (s ^ 2))
        for p in range(pair_count)
        for s in range(sigma_count)
    ]
    return keep + lax.ppermute(away, ("pair", "sigma"), moves)


def y_parts(block):
    return lax.all_to_all(block, "pair", 0, 0, axis_index_groups=Y_GROUPS, tiled=True)


def added(parts, rows=slice(None)):
    return (parts[0, rows] + parts[1, rows]) + (parts[2, rows] + parts[3, rows])


def z_sum(far, up, down, keep, above, below):
    rows = keep.shape[0]

    def send(part, dz):
        return lax.ppermute(part, "pair", z_perm(dz))

    far, up, down = send(far, -2), send(up, 1), send(down, -1)
    above = send(above + up[rows:], 2)
    below = send(below + down[rows:] + far, -2)
    return (keep + up[:rows] + down[:rows]) + (above + below)


def spots():
    position = lax.axis_index("pair")
    x = position // (NZ * NY)
    return lax.axis_index("sigma") ^ (2 * x), x, (position // NY) & (NZ - 1)


def chi_streams(pairs, bins, table, first, streams):
    pair_local, width = pairs.shape
    col_count = width // QUARTERS
    row_count = width // (NX * NZ * NY)
    total = COLUMNS * len(streams)
    shapes = [shape for stream, _ in streams for shape in stream]

    def body(pairs_ref, bins_ref, table_ref, *refs):
        pair_ref, scaled_ref, rows_ref, done = refs[len(shapes) :]
        quarter, x, z = spots()

        def first_column(step):
            return pl.multiple_of(((quarter + step) & (QUARTERS - 1)) * col_count, 128)

        def fetch(step):
            part = pairs_ref.at[:, pl.ds(first_column(step), col_count)]
            return pltpu.make_async_copy(part, pair_ref.at[step], done.at[step])

        for step in range(QUARTERS):
            fetch(step).start()
        index = bins_ref[...]
        upper = lax.broadcasted_iota(jnp.int32, index.shape, 0) > 0
        picked = jnp.zeros(index.shape, jnp.float32)
        for level in range(table.shape[1]):
            picked = jnp.where(index == level, jnp.where(upper, table_ref[1, level], table_ref[0, level]), picked)
        weight = picked / jnp.float32(pair_local * NX * NZ * NY)
        by_pair = jnp.transpose(jnp.concatenate([weight, jnp.zeros((6, pair_local), jnp.float32)], axis=0))
        fetch(0).wait()
        for t in range(total // 128):
            f, column = divmod(first + 128 * t, col_count)
            product = by_pair[:, f : f + 1] * pair_ref[0, :, column : column + 128].astype(jnp.float32)
            scaled_ref[:, 128 * t : 128 * t + 128] = product.astype(jnp.bfloat16)
        for step in range(QUARTERS):
            if step:
                fetch(step).wait()
            rows_ref[pl.ds(first_column(step), col_count), :] = lax.dot_general(
                pair_ref[step], scaled_ref[...], (((0,), (0,)), ((), ())), preferred_element_type=jnp.float32
            )
        before = 0
        for k, (stream, stores) in enumerate(streams):
            for out, index, (left, right), keeps, dz, y in stores:
                at = ((x if keeps else 1 - x) * NZ + ((z + dz) & (NZ - 1))) * NY + y
                rows = pl.ds(pl.multiple_of(at * row_count, 8), row_count)
                refs[before + out][index] = rows_ref[rows, k * COLUMNS + left : k * COLUMNS + right]
            before += len(stream)

    outs = pl.pallas_call(
        body,
        in_specs=[
            pl.BlockSpec(memory_space=pltpu.HBM),
            pl.BlockSpec(memory_space=pltpu.VMEM),
            pl.BlockSpec(memory_space=pltpu.SMEM),
        ],
        out_specs=[pl.BlockSpec(memory_space=pltpu.VMEM)] * len(shapes),
        out_shape=[jax.ShapeDtypeStruct(shape, jnp.float32) for shape in shapes],
        scratch_shapes=[
            pltpu.VMEM((QUARTERS, pair_local, col_count), jnp.bfloat16),
            pltpu.VMEM((pair_local, total), jnp.bfloat16),
            pltpu.VMEM((width, total), jnp.float32),
            pltpu.SemaphoreType.DMA((QUARTERS,)),
        ],
        compiler_params=pltpu.CompilerParams(vmem_limit_bytes=36 << 20),
    )(pltpu.with_memory_space_constraint(pairs, pltpu.HBM), bins, table)
    split = []
    for stream, _ in streams:
        split.append(outs[: len(stream)])
        outs = outs[len(stream) :]
    return split


def local(pair_density_matrices, energy_bins, bin_weights, coulomb, state_matrices):
    width = pair_density_matrices.shape[1]
    pair_count = lax.axis_size("pair")
    sigma_count = lax.axis_size("sigma")
    row_count = width // pair_count
    col_count = width // sigma_count
    pair_position = lax.axis_index("pair")
    quarter = spots()[0]
    rc, n = row_count, COLUMNS
    every = (0, n)
    slots = [(y, keeps, k) for y in range(NY) for keeps in (0, 1) for k in range(NZ)]

    def block(k):
        return slice(k * rc, k * rc + rc)

    b_stores = [(0, (y, block(keeps * NZ + k)), every, keeps, Z_ORDER[k], y) for y, keeps, k in slots]
    c_stores = [(keeps, (block(y * NZ + k),), every, keeps, Z_ORDER[k], y) for y, keeps, k in slots]
    a_stores = []
    for y, keeps, k in slots:
        out, (low, _) = next((j, span) for j, span in enumerate(Z_SLICES) if span[0] <= k < span[1])
        a_stores.append((out, (block(((k - low) * NY + y) * NX + keeps),), every, keeps, Z_ORDER[k], y))

    def streams(first, parts):
        return chi_streams(pair_density_matrices, energy_bins.T, bin_weights, first, parts)

    (b,), c = streams(0, [([(NY, NX * NZ * rc, n)], b_stores), ([(NY * NZ * rc, n)] * 2, c_stores)])
    (a,) = streams(2 * n, [([((high - low) * NY * NX * rc, n) for low, high in Z_SLICES], a_stores)])

    c = x_swap(*c)
    b = y_parts(b)
    b = x_swap(added(b, slice(0, NZ * rc)), added(b, slice(NZ * rc, None)))
    c = y_parts(c.reshape(NY, NZ * rc, n))
    bc = []
    for low, high in Z_SLICES:
        for k in range(low, high):
            bc.append(jnp.concatenate([b[block(k)], added(c, block(k))], axis=0))
    bc = lax.optimization_barrier(
        (bc[0], jnp.concatenate(bc[1:3]), jnp.concatenate(bc[3:5]), bc[5], bc[6], bc[7])
    )
    bc = z_sum(*bc)
    a = z_sum(*a).reshape(NY, NX * rc, n)
    a = y_parts(a)
    a = x_swap(added(a, slice(0, rc)), added(a, slice(rc, None)))
    polar = jnp.concatenate([bc[:rc], bc[rc:], a], axis=1)

    root = jnp.sqrt(coulomb)
    root_rows = lax.dynamic_slice_in_dim(root, pair_position * row_count, row_count, 0)
    root_columns = lax.dynamic_slice_in_dim(root, quarter * col_count, col_count, 0)
    screened = -root_rows[:, None, None] * polar.reshape(row_count, -1, col_count) * root_columns[None, None, :]
    parts = [screened] + [
        lax.ppermute(screened, "sigma", [(s, s ^ k) for s in range(sigma_count)]) for k in range(1, sigma_count)
    ]
    for bit in (1, 2):
        odd = (quarter & bit) != 0
        parts = [jnp.where(odd, parts[k ^ bit], parts[k]) for k in range(sigma_count)]
    states_wide = state_matrices.astype(jnp.float32)
    applied = jnp.einsum(
        "rfc,cn->rfn", jnp.concatenate(parts, axis=2), states_wide, precision=lax.Precision.HIGHEST
    )
    own_states = lax.dynamic_slice_in_dim(states_wide, pair_position * row_count, row_count, 0)
    total = jnp.sum(own_states[:, None, :] * applied, axis=0) / jnp.float32(width)
    spread = jnp.broadcast_to(total.reshape(8, -1)[None], (pair_count, 8, total.size // 8))
    total = jnp.sum(lax.all_to_all(spread, "pair", 0, 0, tiled=True), axis=0).reshape(total.shape)
    return (applied, total)


def solution(mesh):
    return jax.shard_map(
        local,
        mesh=mesh,
        in_specs=(P("pair", None), P("pair", None), P(), P(), P(None, "sigma")),
        out_specs=(P("pair", None, "sigma"), P(None, "sigma")),
        check_vma=False,
    )
```

```python
import jax
import jax.numpy as jnp
from jax import lax
from jax.experimental import pallas as pl
from jax.experimental.pallas import tpu as pltpu
from jax.sharding import PartitionSpec as P


NX, NZ, NY = 2, 8, 4
COLUMNS = 256
QUARTERS = 4
Z_ORDER = (4, 1, 3, -1, -3, 0, 2, -2)
Z_SLICES = ((0, 1), (1, 3), (3, 5), (5, 6), (6, 7), (7, 8))
Y_GROUPS = [[base + y for y in range(NY)] for base in range(0, NX * NZ * NY, NY)]


def place(position):
    return position // (NZ * NY), position // NY % NZ, position % NY


def z_perm(dz):
    moves = []
    for position in range(NX * NZ * NY):
        x, z, y = place(position)
        moves.append((position, (x * NZ + (z + dz) % NZ) * NY + y))
    return moves


def x_swap(away, keep):
    pair_count, sigma_count = lax.axis_size("pair"), lax.axis_size("sigma")
    moves = [
        (p * sigma_count + s, (p ^ (NZ * NY)) * sigma_count + (s ^ 2))
        for p in range(pair_count)
        for s in range(sigma_count)
    ]
    return keep + lax.ppermute(away, ("pair", "sigma"), moves)


def y_parts(block):
    return lax.all_to_all(block, "pair", 0, 0, axis_index_groups=Y_GROUPS, tiled=True)


def added(parts, rows=slice(None)):
    return (parts[0, rows] + parts[1, rows]) + (parts[2, rows] + parts[3, rows])


def z_send(part, dz):
    return lax.ppermute(part, "pair", z_perm(dz))


def z_sum(far, up, down, keep, above, below):
    rows = keep.shape[0]
    far, up, down = z_send(far, -2), z_send(up, 1), z_send(down, -1)
    above = z_send(above + up[rows:], 2)
    below = z_send(below + down[rows:] + far, -2)
    return (keep + up[:rows] + down[:rows]) + (above + below)


def z_sum_both(low, high, up, down, keep, above, below):
    rows, columns = keep.shape
    half = rows // 2
    low, high = z_send(low, -2), z_send(high, 2)
    up, down = z_send(up, 1), z_send(down, -1)

    def middle(low, high, up, down, keep, above, below, above_out, below_out, keep_out):
        above_out[:half] = above[:half] + up[rows : rows + half]
        above_out[half:] = (above[half:] + up[rows + half :]) + high[...]
        below_out[:half] = (below[:half] + down[rows : rows + half]) + low[...]
        below_out[half:] = below[half:] + down[rows + half :]
        keep_out[...] = (keep[...] + up[:rows]) + down[:rows]

    keep, above, below = (pltpu.with_memory_space_constraint(part, pltpu.HBM) for part in (keep, above, below))
    above, below, keep = on_chip(middle, [(rows, columns)] * 3)(low, high, up, down, keep, above, below)
    above, below = z_send(above, 2), z_send(below, -2)

    def last(above, below, keep, out):
        out[...] = keep[...] + (above[...] + below[...])

    return on_chip(last, [(rows, columns)])(above, below, keep)[0]


def on_chip(body, shapes):
    return pl.pallas_call(
        body,
        out_shape=[jax.ShapeDtypeStruct(shape, jnp.float32) for shape in shapes],
        compiler_params=pltpu.CompilerParams(vmem_limit_bytes=12 << 20),
    )


def halves_added(parts):
    half = parts.shape[1] // 2

    def body(parts, first, second):
        first[...] = added(parts, slice(0, half))
        second[...] = added(parts, slice(half, None))

    return on_chip(body, [(half, parts.shape[2])] * 2)(parts)


def spots():
    position = lax.axis_index("pair")
    x = position // (NZ * NY)
    return lax.axis_index("sigma") ^ (2 * x), x, (position // NY) & (NZ - 1)


def fetcher(pairs_ref, pair_ref, done):
    col_count = pair_ref.shape[2]
    quarter = spots()[0]

    def first_column(step):
        return pl.multiple_of(((quarter + step) & (QUARTERS - 1)) * col_count, 128)

    def fetch(step):
        part = pairs_ref.at[:, pl.ds(first_column(step), col_count)]
        return pltpu.make_async_copy(part, pair_ref.at[step], done.at[step])

    return first_column, fetch


def multiply(first_column, fetch, pair_ref, scaled_ref, rows_ref, waited):
    for step in range(QUARTERS):
        if step >= waited:
            fetch(step).wait()
        rows_ref[pl.ds(first_column(step), pair_ref.shape[2]), :] = lax.dot_general(
            pair_ref[step],
            scaled_ref[:, : rows_ref.shape[1]],
            (((0,), (0,)), ((), ())),
            preferred_element_type=jnp.float32,
        )


def store(streams, outs, rows_ref):
    _, x, z = spots()
    before = 0
    for k, (stream, stores) in enumerate(streams):
        for out, index, keeps, dz, y in stores:
            at = ((x if keeps else 1 - x) * NZ + ((z + dz) & (NZ - 1))) * NY + y
            row_count = rows_ref.shape[0] // (NX * NZ * NY)
            rows = pl.ds(pl.multiple_of(at * row_count, 8), row_count)
            outs[before + out][index] = rows_ref[rows, k * COLUMNS : k * COLUMNS + COLUMNS]
        before += len(stream)


def first_streams(pairs, bins, table, streams):
    pair_local, width = pairs.shape
    col_count = width // QUARTERS
    total = 2 * col_count
    now = COLUMNS * len(streams)
    shapes = [shape for stream, _ in streams for shape in stream]
    count = len(shapes)

    def body(pairs_ref, bins_hbm, table_hbm, *refs):
        later_ref, bins_ref, table_ref, pair_ref, scaled_ref, rows_ref, done, small = refs[count:]
        first_column, fetch = fetcher(pairs_ref, pair_ref, done)
        bins_copy = pltpu.make_async_copy(bins_hbm, bins_ref, small.at[0])
        table_copy = pltpu.make_async_copy(table_hbm, table_ref, small.at[1])
        bins_copy.start()
        table_copy.start()
        for step in range(QUARTERS):
            fetch(step).start()
        bins_copy.wait()
        table_copy.wait()
        index = bins_ref[...]
        upper = lax.broadcasted_iota(jnp.int32, index.shape, 0) > 0
        picked = jnp.zeros(index.shape, jnp.float32)
        for level in range(table.shape[1]):
            picked = jnp.where(index == level, jnp.where(upper, table_ref[1, level], table_ref[0, level]), picked)
        weight = picked / jnp.float32(pair_local * NX * NZ * NY)
        by_pair = jnp.transpose(jnp.concatenate([weight, jnp.zeros((6, pair_local), jnp.float32)], axis=0))
        fetch(0).wait()

        def scaled(t):
            f, column = divmod(128 * t, col_count)
            product = by_pair[:, f : f + 1] * pair_ref[0, :, column : column + 128].astype(jnp.float32)
            return product.astype(jnp.bfloat16)

        for t in range(now // 128):
            scaled_ref[:, 128 * t : 128 * t + 128] = scaled(t)
        multiply(first_column, fetch, pair_ref, scaled_ref, rows_ref, 1)
        for t in range(now // 128, total // 128):
            later_ref[:, 128 * t - now : 128 * t - now + 128] = scaled(t)
        store(streams, refs, rows_ref)

    held = [pltpu.with_memory_space_constraint(array, pltpu.HBM) for array in (pairs, bins, table)]
    outs = pl.pallas_call(
        body,
        in_specs=[pl.BlockSpec(memory_space=pltpu.HBM)] * 3,
        out_specs=[pl.BlockSpec(memory_space=pltpu.VMEM)] * (count + 1),
        out_shape=[jax.ShapeDtypeStruct(shape, jnp.float32) for shape in shapes]
        + [jax.ShapeDtypeStruct((pair_local, total - now), jnp.bfloat16)],
        scratch_shapes=[
            pltpu.VMEM(bins.shape, jnp.int32),
            pltpu.SMEM(table.shape, jnp.float32),
            pltpu.VMEM((QUARTERS, pair_local, col_count), jnp.bfloat16),
            pltpu.VMEM((pair_local, now), jnp.bfloat16),
            pltpu.VMEM((width, now), jnp.float32),
            pltpu.SemaphoreType.DMA((QUARTERS,)),
            pltpu.SemaphoreType.DMA((2,)),
        ],
        compiler_params=pltpu.CompilerParams(vmem_limit_bytes=36 << 20),
    )(*held)
    return outs[:-1], outs[-1]


def last_stream(pairs, scaled, stream):
    pair_local, width = pairs.shape
    columns = scaled.shape[1]
    shapes = stream[0]

    def body(pairs_ref, scaled_ref, *refs):
        pair_ref, rows_ref, done = refs[len(shapes) :]
        first_column, fetch = fetcher(pairs_ref, pair_ref, done)
        for step in range(QUARTERS):
            fetch(step).start()
        multiply(first_column, fetch, pair_ref, scaled_ref, rows_ref, 0)
        store([stream], refs, rows_ref)

    return pl.pallas_call(
        body,
        in_specs=[pl.BlockSpec(memory_space=pltpu.HBM), pl.BlockSpec(memory_space=pltpu.VMEM)],
        out_specs=[pl.BlockSpec(shape, lambda: (0, 0)) for shape in shapes],
        out_shape=[pltpu.HBM(shape, jnp.float32) for shape in shapes],
        scratch_shapes=[
            pltpu.VMEM((QUARTERS, pair_local, width // QUARTERS), jnp.bfloat16),
            pltpu.VMEM((width, columns), jnp.float32),
            pltpu.SemaphoreType.DMA((QUARTERS,)),
        ],
        compiler_params=pltpu.CompilerParams(vmem_limit_bytes=24 << 20),
    )(pltpu.with_memory_space_constraint(pairs, pltpu.HBM), scaled)


def local(pair_density_matrices, energy_bins, bin_weights, coulomb, state_matrices):
    width = pair_density_matrices.shape[1]
    pair_count = lax.axis_size("pair")
    sigma_count = lax.axis_size("sigma")
    row_count = width // pair_count
    col_count = width // sigma_count
    pair_position = lax.axis_index("pair")
    quarter = spots()[0]
    rc, n = row_count, COLUMNS
    slots = [(y, keeps, k) for y in range(NY) for keeps in (0, 1) for k in range(NZ)]

    def block(k):
        return slice(k * rc, k * rc + rc)

    b_stores = [(0, (y, block(keeps * NZ + k)), keeps, Z_ORDER[k], y) for y, keeps, k in slots]
    c_stores = [(keeps, (block(y * NZ + k),), keeps, Z_ORDER[k], y) for y, keeps, k in slots]
    a_shapes = [(NY * NX * rc // 2, n)] * 2
    a_shapes += [((high - low) * NY * NX * rc, n) for low, high in Z_SLICES[1:]]
    a_stores = []
    for y, keeps, k in slots:
        if k == 0:
            out, row = divmod(y * NX + keeps, NY * NX // 2)
        else:
            out, (low, _) = next((j, span) for j, span in enumerate(Z_SLICES) if span[0] <= k < span[1])
            out, row = out + 1, ((k - low) * NY + y) * NX + keeps
        a_stores.append((out, (block(row),), keeps, Z_ORDER[k], y))

    (b, *c), scaled = first_streams(
        pair_density_matrices,
        energy_bins.T,
        bin_weights,
        [([(NY, NX * NZ * rc, n)], b_stores), ([(NY * NZ * rc, n)] * 2, c_stores)],
    )
    a = last_stream(pair_density_matrices, scaled, (a_shapes, a_stores))

    c = x_swap(*c)
    b = y_parts(b)
    b = x_swap(*halves_added(b))
    c = y_parts(c.reshape(NY, NZ * rc, n))
    bc = []
    for low, high in Z_SLICES:
        for k in range(low, high):
            bc.append(jnp.concatenate([b[block(k)], added(c, block(k))], axis=0))
    bc = lax.optimization_barrier(
        (bc[0], jnp.concatenate(bc[1:3]), jnp.concatenate(bc[3:5]), bc[5], bc[6], bc[7])
    )
    bc = z_sum(*bc)
    a = z_sum_both(*a).reshape(NY, NX * rc, n)
    a = y_parts(a)
    a = x_swap(added(a, slice(0, rc)), added(a, slice(rc, None)))
    polar = jnp.concatenate([bc[:rc], bc[rc:], a], axis=1)

    root = jnp.sqrt(coulomb)
    root_rows = lax.dynamic_slice_in_dim(root, pair_position * row_count, row_count, 0)
    root_columns = lax.dynamic_slice_in_dim(root, quarter * col_count, col_count, 0)
    screened = -root_rows[:, None, None] * polar.reshape(row_count, -1, col_count) * root_columns[None, None, :]
    parts = [screened] + [
        lax.ppermute(screened, "sigma", [(s, s ^ k) for s in range(sigma_count)]) for k in range(1, sigma_count)
    ]
    for bit in (1, 2):
        odd = (quarter & bit) != 0
        parts = [jnp.where(odd, parts[k ^ bit], parts[k]) for k in range(sigma_count)]
    states_wide = state_matrices.astype(jnp.float32)
    applied = jnp.einsum(
        "rfc,cn->rfn", jnp.concatenate(parts, axis=2), states_wide, precision=lax.Precision.HIGHEST
    )
    own_states = lax.dynamic_slice_in_dim(states_wide, pair_position * row_count, row_count, 0)
    total = jnp.sum(own_states[:, None, :] * applied, axis=0) / jnp.float32(width)
    spread = jnp.broadcast_to(total.reshape(8, -1)[None], (pair_count, 8, total.size // 8))
    total = jnp.sum(lax.all_to_all(spread, "pair", 0, 0, tiled=True), axis=0).reshape(total.shape)
    return (applied, total)


def solution(mesh):
    return jax.shard_map(
        local,
        mesh=mesh,
        in_specs=(P("pair", None), P("pair", None), P(), P(), P(None, "sigma")),
        out_specs=(P("pair", None, "sigma"), P(None, "sigma")),
        check_vma=False,
    )
```

```python
import jax
import jax.numpy as jnp
from jax import lax
from jax.experimental import pallas as pl
from jax.experimental.pallas import tpu as pltpu
from jax.sharding import PartitionSpec as P


NX, NZ, NY = 2, 8, 4
COLUMNS = 256
QUARTERS = 4
Z_ORDER = (4, 1, 3, -1, -3, 0, 2, -2)
Z_SLICES = ((0, 1), (1, 3), (3, 5), (5, 6), (6, 7), (7, 8))
X_GROUPS = [list(range(x * NZ * NY, (x + 1) * NZ * NY)) for x in range(NX)]
Y_GROUPS = [[base + y for y in range(NY)] for base in range(0, NX * NZ * NY, NY)]


def place(position):
    return position // (NZ * NY), position // NY % NZ, position % NY


def z_perm(dz):
    moves = []
    for position in range(NX * NZ * NY):
        x, z, y = place(position)
        moves.append((position, (x * NZ + (z + dz) % NZ) * NY + y))
    return moves


def x_swap(away, keep):
    pair_count, sigma_count = lax.axis_size("pair"), lax.axis_size("sigma")
    moves = [
        (p * sigma_count + s, (p ^ (NZ * NY)) * sigma_count + (s ^ 2))
        for p in range(pair_count)
        for s in range(sigma_count)
    ]
    return keep + lax.ppermute(away, ("pair", "sigma"), moves)


def y_parts(block):
    return lax.all_to_all(block, "pair", 0, 0, axis_index_groups=Y_GROUPS, tiled=True)


def added(parts, rows=slice(None)):
    return (parts[0, rows] + parts[1, rows]) + (parts[2, rows] + parts[3, rows])


def z_send(part, dz):
    return lax.ppermute(part, "pair", z_perm(dz))


def z_sum(far, up, down, keep, above, below):
    rows = keep.shape[0]
    far, up, down = z_send(far, -2), z_send(up, 1), z_send(down, -1)
    above = z_send(above + up[rows:], 2)
    below = z_send(below + down[rows:] + far, -2)
    return (keep + up[:rows] + down[:rows]) + (above + below)


def z_sum_both(low, high, up, down, keep, above, below):
    rows, columns = keep.shape
    half = rows // 2
    low, high = z_send(low, -2), z_send(high, 2)
    up, down = z_send(up, 1), z_send(down, -1)

    def middle(low, high, up, down, keep, above, below, above_out, below_out, keep_out):
        above_out[:half] = above[:half] + up[rows : rows + half]
        above_out[half:] = (above[half:] + up[rows + half :]) + high[...]
        below_out[:half] = (below[:half] + down[rows : rows + half]) + low[...]
        below_out[half:] = below[half:] + down[rows + half :]
        keep_out[...] = (keep[...] + up[:rows]) + down[:rows]

    keep, above, below = (pltpu.with_memory_space_constraint(part, pltpu.HBM) for part in (keep, above, below))
    above, below, keep = on_chip(middle, [(rows, columns)] * 3)(low, high, up, down, keep, above, below)
    above, below = z_send(above, 2), z_send(below, -2)

    def last(above, below, keep, out):
        out[...] = keep[...] + (above[...] + below[...])

    return on_chip(last, [(rows, columns)])(above, below, keep)[0]


def on_chip(body, shapes):
    return pl.pallas_call(
        body,
        out_shape=[jax.ShapeDtypeStruct(shape, jnp.float32) for shape in shapes],
        compiler_params=pltpu.CompilerParams(vmem_limit_bytes=12 << 20),
    )


def halves_added(parts):
    half = parts.shape[1] // 2

    def body(parts, first, second):
        first[...] = added(parts, slice(0, half))
        second[...] = added(parts, slice(half, None))

    return on_chip(body, [(half, parts.shape[2])] * 2)(parts)


def spots():
    position = lax.axis_index("pair")
    x = position // (NZ * NY)
    return lax.axis_index("sigma") ^ (2 * x), x, (position // NY) & (NZ - 1)


def interleaved(one, two, row_count):
    columns = one.shape[1]

    def body(one, two, *outs):
        for out, (low, high) in zip(outs, Z_SLICES):
            for k in range(low, high):
                rows = slice(k * row_count, k * row_count + row_count)
                at = 2 * (k - low) * row_count
                out[at : at + row_count] = one[rows]
                out[at + row_count : at + 2 * row_count] = added(two, rows)

    return on_chip(body, [(2 * (high - low) * row_count, columns) for low, high in Z_SLICES])(one, two)


def fetcher(pairs_ref, pair_ref, done):
    col_count = pair_ref.shape[2]
    quarter = spots()[0]

    def first_column(step):
        return pl.multiple_of(((quarter + step) & (QUARTERS - 1)) * col_count, 128)

    def fetch(step):
        part = pairs_ref.at[:, pl.ds(first_column(step), col_count)]
        return pltpu.make_async_copy(part, pair_ref.at[step], done.at[step])

    return first_column, fetch


def multiply(first_column, fetch, pair_ref, scaled_ref, rows_ref, waited):
    for step in range(QUARTERS):
        if step >= waited:
            fetch(step).wait()
        rows_ref[pl.ds(first_column(step), pair_ref.shape[2]), :] = lax.dot_general(
            pair_ref[step],
            scaled_ref[:, : rows_ref.shape[1]],
            (((0,), (0,)), ((), ())),
            preferred_element_type=jnp.float32,
        )


def store(streams, outs, rows_ref):
    _, x, z = spots()
    before = 0
    for k, (stream, stores) in enumerate(streams):
        for out, index, keeps, dz, y in stores:
            at = ((x if keeps else 1 - x) * NZ + ((z + dz) & (NZ - 1))) * NY + y
            row_count = rows_ref.shape[0] // (NX * NZ * NY)
            rows = pl.ds(pl.multiple_of(at * row_count, 8), row_count)
            outs[before + out][index] = rows_ref[rows, k * COLUMNS : k * COLUMNS + COLUMNS]
        before += len(stream)


def first_streams(pairs, bins, table, streams):
    pair_local, width = pairs.shape
    col_count = width // QUARTERS
    total = 2 * col_count
    now = COLUMNS * len(streams)
    shapes = [shape for stream, _ in streams for shape in stream]
    count = len(shapes)

    def body(pairs_ref, bins_hbm, table_hbm, *refs):
        later_ref, bins_ref, table_ref, pair_ref, scaled_ref, rows_ref, done, small = refs[count:]
        first_column, fetch = fetcher(pairs_ref, pair_ref, done)
        bins_copy = pltpu.make_async_copy(bins_hbm, bins_ref, small.at[0])
        table_copy = pltpu.make_async_copy(table_hbm, table_ref, small.at[1])
        bins_copy.start()
        table_copy.start()
        for step in range(QUARTERS):
            fetch(step).start()
        bins_copy.wait()
        table_copy.wait()
        index = bins_ref[...]
        upper = lax.broadcasted_iota(jnp.int32, index.shape, 0) > 0
        picked = jnp.zeros(index.shape, jnp.float32)
        for level in range(table.shape[1]):
            picked = jnp.where(index == level, jnp.where(upper, table_ref[1, level], table_ref[0, level]), picked)
        weight = picked / jnp.float32(pair_local * NX * NZ * NY)
        by_pair = jnp.transpose(jnp.concatenate([weight, jnp.zeros((6, pair_local), jnp.float32)], axis=0))
        fetch(0).wait()

        def scaled(t):
            f, column = divmod(128 * t, col_count)
            product = by_pair[:, f : f + 1] * pair_ref[0, :, column : column + 128].astype(jnp.float32)
            return product.astype(jnp.bfloat16)

        for t in range(now // 128):
            scaled_ref[:, 128 * t : 128 * t + 128] = scaled(t)
        multiply(first_column, fetch, pair_ref, scaled_ref, rows_ref, 1)
        for t in range(now // 128, total // 128):
            later_ref[:, 128 * t - now : 128 * t - now + 128] = scaled(t)
        store(streams, refs, rows_ref)

    held = [pltpu.with_memory_space_constraint(array, pltpu.HBM) for array in (pairs, bins, table)]
    outs = pl.pallas_call(
        body,
        in_specs=[pl.BlockSpec(memory_space=pltpu.HBM)] * 3,
        out_specs=[pl.BlockSpec(memory_space=pltpu.VMEM)] * (count + 1),
        out_shape=[jax.ShapeDtypeStruct(shape, jnp.float32) for shape in shapes]
        + [jax.ShapeDtypeStruct((pair_local, total - now), jnp.bfloat16)],
        scratch_shapes=[
            pltpu.VMEM(bins.shape, jnp.int32),
            pltpu.SMEM(table.shape, jnp.float32),
            pltpu.VMEM((QUARTERS, pair_local, col_count), jnp.bfloat16),
            pltpu.VMEM((pair_local, now), jnp.bfloat16),
            pltpu.VMEM((width, now), jnp.float32),
            pltpu.SemaphoreType.DMA((QUARTERS,)),
            pltpu.SemaphoreType.DMA((2,)),
        ],
        compiler_params=pltpu.CompilerParams(vmem_limit_bytes=36 << 20),
    )(*held)
    return outs[:-1], outs[-1]


def last_stream(pairs, scaled, stream):
    pair_local, width = pairs.shape
    columns = scaled.shape[1]
    shapes = stream[0]

    part = pair_local // QUARTERS

    def body(pairs_ref, scaled_ref, *refs):
        pair_ref, turned_ref, sum_ref, rows_ref, done = refs[len(shapes) :]

        def fetch(step):
            return pltpu.make_async_copy(pairs_ref.at[step * part : step * part + part], pair_ref.at[step], done.at[step])

        for step in range(QUARTERS):
            fetch(step).start()
        turned_ref[...] = jnp.transpose(scaled_ref[...])
        for step in range(QUARTERS):
            fetch(step).wait()
            product = jnp.dot(
                turned_ref[:, step * part : step * part + part], pair_ref[step], preferred_element_type=jnp.float32
            )
            if step == 0:
                sum_ref[...] = product
            elif step < QUARTERS - 1:
                sum_ref[...] += product
            else:
                rows_ref[...] = jnp.transpose(sum_ref[...] + product)
        store([stream], refs, rows_ref)

    return pl.pallas_call(
        body,
        in_specs=[pl.BlockSpec(memory_space=pltpu.HBM), pl.BlockSpec(memory_space=pltpu.VMEM)],
        out_specs=[pl.BlockSpec(shape, lambda: (0, 0)) for shape in shapes],
        out_shape=[pltpu.HBM(shape, jnp.float32) for shape in shapes],
        scratch_shapes=[
            pltpu.VMEM((QUARTERS, part, width), jnp.bfloat16),
            pltpu.VMEM((columns, pair_local), jnp.bfloat16),
            pltpu.VMEM((columns, width), jnp.float32),
            pltpu.VMEM((width, columns), jnp.float32),
            pltpu.SemaphoreType.DMA((QUARTERS,)),
        ],
        compiler_params=pltpu.CompilerParams(vmem_limit_bytes=24 << 20),
    )(pltpu.with_memory_space_constraint(pairs, pltpu.HBM), scaled)


def local(pair_density_matrices, energy_bins, bin_weights, coulomb, state_matrices):
    width = pair_density_matrices.shape[1]
    pair_count = lax.axis_size("pair")
    sigma_count = lax.axis_size("sigma")
    row_count = width // pair_count
    col_count = width // sigma_count
    pair_position = lax.axis_index("pair")
    quarter = spots()[0]
    rc, n = row_count, COLUMNS
    slots = [(y, keeps, k) for y in range(NY) for keeps in (0, 1) for k in range(NZ)]

    def block(k):
        return slice(k * rc, k * rc + rc)

    b_stores = [(0, (y, block(keeps * NZ + k)), keeps, Z_ORDER[k], y) for y, keeps, k in slots]
    c_stores = [(keeps, (block(y * NZ + k),), keeps, Z_ORDER[k], y) for y, keeps, k in slots]
    a_shapes = [(NY * NX * rc // 2, n)] * 2
    a_shapes += [((high - low) * NY * NX * rc, n) for low, high in Z_SLICES[1:]]
    a_stores = []
    for y, keeps, k in slots:
        if k == 0:
            out, row = divmod(y * NX + keeps, NY * NX // 2)
        else:
            out, (low, _) = next((j, span) for j, span in enumerate(Z_SLICES) if span[0] <= k < span[1])
            out, row = out + 1, ((k - low) * NY + y) * NX + keeps
        a_stores.append((out, (block(row),), keeps, Z_ORDER[k], y))

    (b, *c), scaled = first_streams(
        pair_density_matrices,
        energy_bins.T,
        bin_weights,
        [([(NY, NX * NZ * rc, n)], b_stores), ([(NY * NZ * rc, n)] * 2, c_stores)],
    )
    a = last_stream(pair_density_matrices, scaled, (a_shapes, a_stores))

    c = x_swap(*c)
    b = y_parts(b)
    b = x_swap(*halves_added(b))
    c = y_parts(c.reshape(NY, NZ * rc, n))
    bc = interleaved(b, c, rc)
    bc = z_sum(*bc)
    a = z_sum_both(*a).reshape(NY, NX * rc, n)
    a = y_parts(a)
    a = x_swap(added(a, slice(0, rc)), added(a, slice(rc, None)))
    polar = jnp.concatenate([bc[:rc], bc[rc:], a], axis=1)

    root = jnp.sqrt(coulomb)
    root_rows = lax.dynamic_slice_in_dim(root, pair_position * row_count, row_count, 0)
    root_columns = lax.dynamic_slice_in_dim(root, quarter * col_count, col_count, 0)
    screened = -root_rows[:, None, None] * polar.reshape(row_count, -1, col_count) * root_columns[None, None, :]
    gathered = lax.all_gather(screened, "sigma")
    upper = quarter != lax.axis_index("sigma")
    parts = [jnp.where(upper, gathered[k ^ 2], gathered[k]) for k in range(sigma_count)]
    states_wide = state_matrices.astype(jnp.float32)
    applied = jnp.einsum(
        "rfc,cn->rfn", jnp.concatenate(parts, axis=2), states_wide, precision=lax.Precision.HIGHEST
    )
    own_states = lax.dynamic_slice_in_dim(states_wide, pair_position * row_count, row_count, 0)
    total = jnp.sum(own_states[:, None, :] * applied, axis=0) / jnp.float32(width)
    tile = total.reshape(8, -1)
    tile += lax.ppermute(tile, "pair", [(p, p ^ (NZ * NY)) for p in range(pair_count)])
    spread = jnp.broadcast_to(tile[None], (NZ * NY,) + tile.shape)
    total = jnp.sum(lax.all_to_all(spread, "pair", 0, 0, axis_index_groups=X_GROUPS, tiled=True), axis=0).reshape(total.shape)
    return (applied, total)


def solution(mesh):
    return jax.shard_map(
        local,
        mesh=mesh,
        in_specs=(P("pair", None), P("pair", None), P(), P(), P(None, "sigma")),
        out_specs=(P("pair", None, "sigma"), P(None, "sigma")),
        check_vma=False,
    )
```

```python
import jax
import jax.numpy as jnp
from jax import lax
from jax.experimental import pallas as pl
from jax.experimental.pallas import tpu as pltpu
from jax.sharding import PartitionSpec as P


NX, NZ, NY = 2, 8, 4
COLUMNS = 256
QUARTERS = 4
Z_ORDER = (4, 1, 3, -1, -3, 0, 2, -2)
Z_SLICES = ((0, 1), (1, 3), (3, 5), (5, 6), (6, 7), (7, 8))
X_GROUPS = [list(range(x * NZ * NY, (x + 1) * NZ * NY)) for x in range(NX)]
Y_GROUPS = [[base + y for y in range(NY)] for base in range(0, NX * NZ * NY, NY)]


def place(position):
    return position // (NZ * NY), position // NY % NZ, position % NY


def z_perm(dz):
    moves = []
    for position in range(NX * NZ * NY):
        x, z, y = place(position)
        moves.append((position, (x * NZ + (z + dz) % NZ) * NY + y))
    return moves


def x_swap(away):
    pair_count, sigma_count = lax.axis_size("pair"), lax.axis_size("sigma")
    moves = [
        (p * sigma_count + s, (p ^ (NZ * NY)) * sigma_count + (s ^ 2))
        for p in range(pair_count)
        for s in range(sigma_count)
    ]
    return lax.ppermute(away, ("pair", "sigma"), moves)


def y_send(part, dy):
    moves = []
    for position in range(NX * NZ * NY):
        x, z, y = place(position)
        moves.append((position, (x * NZ + z) * NY + (y + dy) % NY))
    return lax.ppermute(part, "pair", moves)


def y_parts(block):
    return lax.all_to_all(block, "pair", 0, 0, axis_index_groups=Y_GROUPS, tiled=True)


def added(parts, rows=slice(None)):
    return (parts[0, rows] + parts[1, rows]) + (parts[2, rows] + parts[3, rows])


def z_send(part, dz):
    return lax.ppermute(part, "pair", z_perm(dz))


def z_sum(far, up, down, keep, above, below):
    rows = keep.shape[0]
    far, up, down = z_send(far, -2), z_send(up, 1), z_send(down, -1)
    above = z_send(above + up[rows:], 2)
    below = z_send(below + down[rows:] + far, -2)
    return keep, up, down, above, below


def z_sum_both(low, high, up, down, keep, above, below):
    rows, columns = keep.shape
    half = rows // 2
    low, high = z_send(low, -2), z_send(high, 2)
    up, down = z_send(up, 1), z_send(down, -1)

    def middle(low, high, up, down, keep, above, below, above_out, below_out, keep_out):
        above_out[:half] = above[:half] + up[rows : rows + half]
        above_out[half:] = (above[half:] + up[rows + half :]) + high[...]
        below_out[:half] = (below[:half] + down[rows : rows + half]) + low[...]
        below_out[half:] = below[half:] + down[rows + half :]
        keep_out[...] = (keep[...] + up[:rows]) + down[:rows]

    keep, above, below = (pltpu.with_memory_space_constraint(part, pltpu.HBM) for part in (keep, above, below))
    above, below, keep = on_chip(middle, [(rows, columns)] * 3)(low, high, up, down, keep, above, below)
    above, below = z_send(above, 2), z_send(below, -2)

    def last(above, below, keep, out):
        out[...] = keep[...] + (above[...] + below[...])

    return on_chip(last, [(rows, columns)])(above, below, keep)[0]


def on_chip(body, shapes):
    return pl.pallas_call(
        body,
        out_shape=[jax.ShapeDtypeStruct(shape, jnp.float32) for shape in shapes],
        compiler_params=pltpu.CompilerParams(vmem_limit_bytes=12 << 20),
    )


def halves_added(parts):
    half = parts.shape[1] // 2

    def body(parts, first, second):
        first[...] = added(parts, slice(0, half))
        second[...] = added(parts, slice(half, None))

    return on_chip(body, [(half, parts.shape[2])] * 2)(parts)


def spots():
    position = lax.axis_index("pair")
    x = position // (NZ * NY)
    return lax.axis_index("sigma") ^ (2 * x), x, (position // NY) & (NZ - 1), position & (NY - 1)


def x_added(keep, other):
    rows = keep.shape[0] // NY

    def body(keep, other, *outs):
        for k, out in enumerate(outs):
            out[...] = keep[k * rows : k * rows + rows] + other[k * rows : k * rows + rows]

    return on_chip(body, [(rows, keep.shape[1])] * NY)(keep, other)


def interleaved(keep, other, two, row_count):
    columns = keep.shape[1]

    def body(keep, other, *refs):
        two, outs = refs[:NY], refs[NY:]
        for out, (low, high) in zip(outs, Z_SLICES):
            for k in range(low, high):
                rows = slice(k * row_count, k * row_count + row_count)
                at = 2 * (k - low) * row_count
                out[at : at + row_count] = keep[rows] + other[rows]
                out[at + row_count : at + 2 * row_count] = (two[0][rows] + two[1][rows]) + (two[2][rows] + two[3][rows])

    return on_chip(body, [(2 * (high - low) * row_count, columns) for low, high in Z_SLICES])(keep, other, *two)


def screened_block(ring, keep, other, root_rows, root_columns):
    rows, columns = keep.shape

    def body(kept, up, down, above, below, keep, other, by_row, by_column, out):
        for k in range(2):
            part = slice(k * rows, k * rows + rows)
            total = ((kept[part] + up[part]) + down[part]) + (above[part] + below[part])
            span = slice(k * columns, k * columns + columns)
            out[:, span] = by_row[...] * total * by_column[:, span]
        out[:, 2 * columns :] = by_row[...] * (keep[...] + other[...]) * by_column[:, 2 * columns :]

    return on_chip(body, [(rows, 3 * columns)])(*ring, keep, other, root_rows, root_columns)[0]


def fetcher(pairs_ref, pair_ref, done):
    col_count = pair_ref.shape[2]
    quarter = spots()[0]

    def first_column(step):
        return pl.multiple_of(((quarter + step) & (QUARTERS - 1)) * col_count, 128)

    def fetch(step):
        part = pairs_ref.at[:, pl.ds(first_column(step), col_count)]
        return pltpu.make_async_copy(part, pair_ref.at[step], done.at[step])

    return first_column, fetch


def multiply(first_column, fetch, pair_ref, scaled_ref, rows_ref, waited):
    for step in range(QUARTERS):
        if step >= waited:
            fetch(step).wait()
        rows_ref[pl.ds(first_column(step), pair_ref.shape[2]), :] = lax.dot_general(
            pair_ref[step],
            scaled_ref[:, : rows_ref.shape[1]],
            (((0,), (0,)), ((), ())),
            preferred_element_type=jnp.float32,
        )


def store(streams, outs, rows_ref):
    _, x, z, own_y = spots()
    before = 0
    for k, (stream, stores) in enumerate(streams):
        for out, index, keeps, dz, y in stores:
            y = y if y >= 0 else (own_y - y) & (NY - 1)
            at = ((x if keeps else 1 - x) * NZ + ((z + dz) & (NZ - 1))) * NY + y
            row_count = rows_ref.shape[0] // (NX * NZ * NY)
            rows = pl.ds(pl.multiple_of(at * row_count, 8), row_count)
            outs[before + out][index] = rows_ref[rows, k * COLUMNS : k * COLUMNS + COLUMNS]
        before += len(stream)


def first_streams(pairs, bins, table, streams):
    pair_local, width = pairs.shape
    col_count = width // QUARTERS
    total = 2 * col_count
    now = COLUMNS * len(streams)
    shapes = [shape for stream, _ in streams for shape in stream]
    count = len(shapes)

    def body(pairs_ref, bins_hbm, table_hbm, *refs):
        later_ref, bins_ref, table_ref, pair_ref, scaled_ref, rows_ref, done, small = refs[count:]
        first_column, fetch = fetcher(pairs_ref, pair_ref, done)
        bins_copy = pltpu.make_async_copy(bins_hbm, bins_ref, small.at[0])
        table_copy = pltpu.make_async_copy(table_hbm, table_ref, small.at[1])
        bins_copy.start()
        table_copy.start()
        for step in range(QUARTERS):
            fetch(step).start()
        bins_copy.wait()
        table_copy.wait()
        index = bins_ref[...]
        upper = lax.broadcasted_iota(jnp.int32, index.shape, 0) > 0
        picked = jnp.zeros(index.shape, jnp.float32)
        for level in range(table.shape[1]):
            picked = jnp.where(index == level, jnp.where(upper, table_ref[1, level], table_ref[0, level]), picked)
        weight = picked / jnp.float32(pair_local * NX * NZ * NY)
        by_pair = jnp.transpose(jnp.concatenate([weight, jnp.zeros((6, pair_local), jnp.float32)], axis=0))
        fetch(0).wait()

        def scaled(t):
            f, column = divmod(128 * t, col_count)
            product = by_pair[:, f : f + 1] * pair_ref[0, :, column : column + 128].astype(jnp.float32)
            return product.astype(jnp.bfloat16)

        for t in range(now // 128):
            scaled_ref[:, 128 * t : 128 * t + 128] = scaled(t)
        multiply(first_column, fetch, pair_ref, scaled_ref, rows_ref, 1)
        for t in range(now // 128, total // 128):
            later_ref[:, 128 * t - now : 128 * t - now + 128] = scaled(t)
        store(streams, refs, rows_ref)

    held = [pltpu.with_memory_space_constraint(array, pltpu.HBM) for array in (pairs, bins, table)]
    outs = pl.pallas_call(
        body,
        in_specs=[pl.BlockSpec(memory_space=pltpu.HBM)] * 3,
        out_specs=[pl.BlockSpec(memory_space=pltpu.VMEM)] * (count + 1),
        out_shape=[jax.ShapeDtypeStruct(shape, jnp.float32) for shape in shapes]
        + [jax.ShapeDtypeStruct((pair_local, total - now), jnp.bfloat16)],
        scratch_shapes=[
            pltpu.VMEM(bins.shape, jnp.int32),
            pltpu.SMEM(table.shape, jnp.float32),
            pltpu.VMEM((QUARTERS, pair_local, col_count), jnp.bfloat16),
            pltpu.VMEM((pair_local, now), jnp.bfloat16),
            pltpu.VMEM((width, now), jnp.float32),
            pltpu.SemaphoreType.DMA((QUARTERS,)),
            pltpu.SemaphoreType.DMA((2,)),
        ],
        compiler_params=pltpu.CompilerParams(vmem_limit_bytes=36 << 20),
    )(*held)
    return outs[:-1], outs[-1]


def last_stream(pairs, scaled, stream):
    pair_local, width = pairs.shape
    columns = scaled.shape[1]
    shapes = stream[0]

    part = pair_local // QUARTERS

    def body(pairs_ref, scaled_ref, *refs):
        pair_ref, turned_ref, sum_ref, rows_ref, done = refs[len(shapes) :]

        def fetch(step):
            return pltpu.make_async_copy(pairs_ref.at[step * part : step * part + part], pair_ref.at[step], done.at[step])

        for step in range(QUARTERS):
            fetch(step).start()
        turned_ref[...] = jnp.transpose(scaled_ref[...])
        for step in range(QUARTERS):
            fetch(step).wait()
            product = jnp.dot(
                turned_ref[:, step * part : step * part + part], pair_ref[step], preferred_element_type=jnp.float32
            )
            if step == 0:
                sum_ref[...] = product
            elif step < QUARTERS - 1:
                sum_ref[...] += product
            else:
                rows_ref[...] = jnp.transpose(sum_ref[...] + product)
        store([stream], refs, rows_ref)

    return pl.pallas_call(
        body,
        in_specs=[pl.BlockSpec(memory_space=pltpu.HBM), pl.BlockSpec(memory_space=pltpu.VMEM)],
        out_specs=[pl.BlockSpec(shape, lambda: (0, 0)) for shape in shapes],
        out_shape=[pltpu.HBM(shape, jnp.float32) for shape in shapes],
        scratch_shapes=[
            pltpu.VMEM((QUARTERS, part, width), jnp.bfloat16),
            pltpu.VMEM((columns, pair_local), jnp.bfloat16),
            pltpu.VMEM((columns, width), jnp.float32),
            pltpu.VMEM((width, columns), jnp.float32),
            pltpu.SemaphoreType.DMA((QUARTERS,)),
        ],
        compiler_params=pltpu.CompilerParams(vmem_limit_bytes=24 << 20),
    )(pltpu.with_memory_space_constraint(pairs, pltpu.HBM), scaled)


def local(pair_density_matrices, energy_bins, bin_weights, coulomb, state_matrices):
    width = pair_density_matrices.shape[1]
    pair_count = lax.axis_size("pair")
    sigma_count = lax.axis_size("sigma")
    row_count = width // pair_count
    col_count = width // sigma_count
    pair_position = lax.axis_index("pair")
    quarter = spots()[0]
    rc, n = row_count, COLUMNS
    slots = [(y, keeps, k) for y in range(NY) for keeps in (0, 1) for k in range(NZ)]

    def block(k):
        return slice(k * rc, k * rc + rc)

    b_stores = [(0, (y, block(keeps * NZ + k)), keeps, Z_ORDER[k], y) for y, keeps, k in slots]
    c_stores = [(keeps, (block(y * NZ + k),), keeps, Z_ORDER[k], -1 - y) for y, keeps, k in slots]
    a_shapes = [(NY * NX * rc // 2, n)] * 2
    a_shapes += [((high - low) * NY * NX * rc, n) for low, high in Z_SLICES[1:]]
    a_stores = []
    for y, keeps, k in slots:
        if k == 0:
            out, row = divmod(y * NX + keeps, NY * NX // 2)
        else:
            out, (low, _) = next((j, span) for j, span in enumerate(Z_SLICES) if span[0] <= k < span[1])
            out, row = out + 1, ((k - low) * NY + y) * NX + keeps
        a_stores.append((out, (block(row),), keeps, Z_ORDER[k], y))

    (b, *c), scaled = first_streams(
        pair_density_matrices,
        energy_bins.T,
        bin_weights,
        [([(NY, NX * NZ * rc, n)], b_stores), ([(NY * NZ * rc, n)] * 2, c_stores)],
    )
    a = last_stream(pair_density_matrices, scaled, (a_shapes, a_stores))

    c = x_added(c[1], x_swap(c[0]))
    c = [c[-1]] + [y_send(c[dy - 1], dy) for dy in (1, 3, 2)]
    b = halves_added(y_parts(b))
    bc = interleaved(b[1], x_swap(b[0]), c, rc)
    bc = z_sum(*bc)
    a = z_sum_both(*a).reshape(NY, NX * rc, n)
    a = y_parts(a)
    a = added(a, slice(0, rc)), added(a, slice(rc, None))
    root = jnp.sqrt(coulomb)
    root_rows = -lax.dynamic_slice_in_dim(root, pair_position * row_count, row_count, 0)
    root_columns = lax.dynamic_slice_in_dim(root, quarter * col_count, col_count, 0)
    root_columns = jnp.concatenate([root_columns, root_columns])
    screened = screened_block(bc, a[1], x_swap(a[0]), root_rows[:, None], root_columns[None, :])
    screened = screened.reshape(row_count, -1, col_count)
    gathered = lax.all_gather(screened, "sigma")
    upper = quarter != lax.axis_index("sigma")
    parts = [jnp.where(upper, gathered[k ^ 2], gathered[k]) for k in range(sigma_count)]
    states_wide = state_matrices.astype(jnp.float32)
    applied = jnp.einsum(
        "rfc,cn->rfn", jnp.concatenate(parts, axis=2), states_wide, precision=lax.Precision.HIGHEST
    )
    own_states = lax.dynamic_slice_in_dim(states_wide, pair_position * row_count, row_count, 0)
    total = jnp.sum(own_states[:, None, :] * applied, axis=0) / jnp.float32(width)
    tile = total.reshape(8, -1)
    tile += lax.ppermute(tile, "pair", [(p, p ^ (NZ * NY)) for p in range(pair_count)])
    spread = jnp.broadcast_to(tile[None], (NZ * NY,) + tile.shape)
    total = jnp.sum(lax.all_to_all(spread, "pair", 0, 0, axis_index_groups=X_GROUPS, tiled=True), axis=0).reshape(total.shape)
    return (applied, total)


def solution(mesh):
    return jax.shard_map(
        local,
        mesh=mesh,
        in_specs=(P("pair", None), P("pair", None), P(), P(), P(None, "sigma")),
        out_specs=(P("pair", None, "sigma"), P(None, "sigma")),
        check_vma=False,
    )
```

```python
import jax
import jax.numpy as jnp
from jax import lax
from jax.experimental import pallas as pl
from jax.experimental.pallas import tpu as pltpu
from jax.sharding import PartitionSpec as P


NX, NZ, NY = 2, 8, 4
COLUMNS = 256
QUARTERS = 4
Z_ORDER = (4, 1, 3, -1, -3, 0, 2, -2)
Z_SLICES = ((0, 1), (1, 3), (3, 5), (5, 6), (6, 7), (7, 8))
X_GROUPS = [list(range(x * NZ * NY, (x + 1) * NZ * NY)) for x in range(NX)]
Y_GROUPS = [[base + y for y in range(NY)] for base in range(0, NX * NZ * NY, NY)]


def place(position):
    return position // (NZ * NY), position // NY % NZ, position % NY


def z_perm(dz):
    moves = []
    for position in range(NX * NZ * NY):
        x, z, y = place(position)
        moves.append((position, (x * NZ + (z + dz) % NZ) * NY + y))
    return moves


def x_swap(away):
    pair_count, sigma_count = lax.axis_size("pair"), lax.axis_size("sigma")
    moves = [
        (p * sigma_count + s, (p ^ (NZ * NY)) * sigma_count + (s ^ 2))
        for p in range(pair_count)
        for s in range(sigma_count)
    ]
    return lax.ppermute(away, ("pair", "sigma"), moves)


def y_send(part, dy):
    moves = []
    for position in range(NX * NZ * NY):
        x, z, y = place(position)
        moves.append((position, (x * NZ + z) * NY + (y + dy) % NY))
    return lax.ppermute(part, "pair", moves)


def y_direct(blocks):
    return [blocks[-1]] + [y_send(blocks[dy - 1], dy) for dy in (1, 3, 2)]


def y_parts(block):
    return lax.all_to_all(block, "pair", 0, 0, axis_index_groups=Y_GROUPS, tiled=True)


def added(parts, rows=slice(None)):
    return (parts[0, rows] + parts[1, rows]) + (parts[2, rows] + parts[3, rows])


def z_send(part, dz):
    return lax.ppermute(part, "pair", z_perm(dz))


def z_sum(far, up, down, keep, above, below):
    rows = keep.shape[0]
    far, up, down = z_send(far, -2), z_send(up, 1), z_send(down, -1)
    above = z_send(above + up[rows:], 2)
    below = z_send(below + down[rows:] + far, -2)
    return keep, up, down, above, below


def z_sum_both(low, high, up, down, keep, above, below):
    rows, columns = keep.shape
    half = rows // 2
    low, high = z_send(low, -2), z_send(high, 2)
    up, down = z_send(up, 1), z_send(down, -1)

    def middle(low, high, up, down, keep, above, below, above_out, below_out, keep_out):
        above_out[:half] = above[:half] + up[rows : rows + half]
        above_out[half:] = (above[half:] + up[rows + half :]) + high[...]
        below_out[:half] = (below[:half] + down[rows : rows + half]) + low[...]
        below_out[half:] = below[half:] + down[rows + half :]
        keep_out[...] = (keep[...] + up[:rows]) + down[:rows]

    keep, above, below = (pltpu.with_memory_space_constraint(part, pltpu.HBM) for part in (keep, above, below))
    above, below, keep = on_chip(middle, [(rows, columns)] * 3)(low, high, up, down, keep, above, below)
    above, below = z_send(above, 2), z_send(below, -2)

    part = rows // NY

    def last(above, below, keep, *outs):
        for k, out in enumerate(outs):
            span = slice(k * part, k * part + part)
            out[...] = keep[span] + (above[span] + below[span])

    return on_chip(last, [(part, columns)] * NY)(above, below, keep)


def on_chip(body, shapes):
    return pl.pallas_call(
        body,
        out_shape=[jax.ShapeDtypeStruct(shape, jnp.float32) for shape in shapes],
        compiler_params=pltpu.CompilerParams(vmem_limit_bytes=12 << 20),
    )


def halves_added(parts):
    half = parts.shape[1] // 2

    def body(parts, first, second):
        first[...] = added(parts, slice(0, half))
        second[...] = added(parts, slice(half, None))

    return on_chip(body, [(half, parts.shape[2])] * 2)(parts)


def spots():
    position = lax.axis_index("pair")
    x = position // (NZ * NY)
    return lax.axis_index("sigma") ^ (2 * x), x, (position // NY) & (NZ - 1), position & (NY - 1)


def x_added(keep, other):
    rows = keep.shape[0] // NY

    def body(keep, other, *outs):
        for k, out in enumerate(outs):
            out[...] = keep[k * rows : k * rows + rows] + other[k * rows : k * rows + rows]

    return on_chip(body, [(rows, keep.shape[1])] * NY)(keep, other)


def interleaved(keep, other, two, row_count):
    columns = keep.shape[1]

    def body(keep, other, *refs):
        two, outs = refs[:NY], refs[NY:]
        for out, (low, high) in zip(outs, Z_SLICES):
            for k in range(low, high):
                rows = slice(k * row_count, k * row_count + row_count)
                at = 2 * (k - low) * row_count
                out[at : at + row_count] = keep[rows] + other[rows]
                out[at + row_count : at + 2 * row_count] = (two[0][rows] + two[1][rows]) + (two[2][rows] + two[3][rows])

    return on_chip(body, [(2 * (high - low) * row_count, columns) for low, high in Z_SLICES])(keep, other, *two)


def screened_block(ring, keep, other, root_rows, root_columns):
    rows, columns = keep.shape

    def body(kept, up, down, above, below, keep, other, by_row, by_column, out):
        for k in range(2):
            part = slice(k * rows, k * rows + rows)
            total = ((kept[part] + up[part]) + down[part]) + (above[part] + below[part])
            span = slice(k * columns, k * columns + columns)
            out[:, span] = by_row[...] * total * by_column[:, span]
        out[:, 2 * columns :] = by_row[...] * (keep[...] + other[...]) * by_column[:, 2 * columns :]

    return on_chip(body, [(rows, 3 * columns)])(*ring, keep, other, root_rows, root_columns)[0]


def fetcher(pairs_ref, pair_ref, done):
    col_count = pair_ref.shape[2]
    quarter = spots()[0]

    def first_column(step):
        return pl.multiple_of(((quarter + step) & (QUARTERS - 1)) * col_count, 128)

    def fetch(step):
        part = pairs_ref.at[:, pl.ds(first_column(step), col_count)]
        return pltpu.make_async_copy(part, pair_ref.at[step], done.at[step])

    return first_column, fetch


def multiply(first_column, fetch, pair_ref, scaled_ref, rows_ref, waited):
    for step in range(QUARTERS):
        if step >= waited:
            fetch(step).wait()
        rows_ref[pl.ds(first_column(step), pair_ref.shape[2]), :] = lax.dot_general(
            pair_ref[step],
            scaled_ref[:, : rows_ref.shape[1]],
            (((0,), (0,)), ((), ())),
            preferred_element_type=jnp.float32,
        )


def store(streams, outs, rows_ref):
    _, x, z, own_y = spots()
    before = 0
    for k, (stream, stores) in enumerate(streams):
        for out, index, keeps, dz, y in stores:
            y = y if y >= 0 else (own_y - y) & (NY - 1)
            at = ((x if keeps else 1 - x) * NZ + ((z + dz) & (NZ - 1))) * NY + y
            row_count = rows_ref.shape[0] // (NX * NZ * NY)
            rows = pl.ds(pl.multiple_of(at * row_count, 8), row_count)
            outs[before + out][index] = rows_ref[rows, k * COLUMNS : k * COLUMNS + COLUMNS]
        before += len(stream)


def first_streams(pairs, bins, table, streams):
    pair_local, width = pairs.shape
    col_count = width // QUARTERS
    total = 2 * col_count
    now = COLUMNS * len(streams)
    shapes = [shape for stream, _ in streams for shape in stream]
    count = len(shapes)

    def body(pairs_ref, bins_hbm, table_hbm, *refs):
        later_ref, bins_ref, table_ref, pair_ref, scaled_ref, rows_ref, done, small = refs[count:]
        first_column, fetch = fetcher(pairs_ref, pair_ref, done)
        bins_copy = pltpu.make_async_copy(bins_hbm, bins_ref, small.at[0])
        table_copy = pltpu.make_async_copy(table_hbm, table_ref, small.at[1])
        bins_copy.start()
        table_copy.start()
        for step in range(QUARTERS):
            fetch(step).start()
        bins_copy.wait()
        table_copy.wait()
        index = bins_ref[...]
        upper = lax.broadcasted_iota(jnp.int32, index.shape, 0) > 0
        picked = jnp.zeros(index.shape, jnp.float32)
        for level in range(table.shape[1]):
            picked = jnp.where(index == level, jnp.where(upper, table_ref[1, level], table_ref[0, level]), picked)
        weight = picked / jnp.float32(pair_local * NX * NZ * NY)
        by_pair = jnp.transpose(jnp.concatenate([weight, jnp.zeros((6, pair_local), jnp.float32)], axis=0))
        fetch(0).wait()

        def scaled(t):
            f, column = divmod(128 * t, col_count)
            product = by_pair[:, f : f + 1] * pair_ref[0, :, column : column + 128].astype(jnp.float32)
            return product.astype(jnp.bfloat16)

        for t in range(now // 128):
            scaled_ref[:, 128 * t : 128 * t + 128] = scaled(t)
        multiply(first_column, fetch, pair_ref, scaled_ref, rows_ref, 1)
        for t in range(now // 128, total // 128):
            later_ref[:, 128 * t - now : 128 * t - now + 128] = scaled(t)
        store(streams, refs, rows_ref)

    held = [pltpu.with_memory_space_constraint(array, pltpu.HBM) for array in (pairs, bins, table)]
    outs = pl.pallas_call(
        body,
        in_specs=[pl.BlockSpec(memory_space=pltpu.HBM)] * 3,
        out_specs=[pl.BlockSpec(memory_space=pltpu.VMEM)] * (count + 1),
        out_shape=[jax.ShapeDtypeStruct(shape, jnp.float32) for shape in shapes]
        + [jax.ShapeDtypeStruct((pair_local, total - now), jnp.bfloat16)],
        scratch_shapes=[
            pltpu.VMEM(bins.shape, jnp.int32),
            pltpu.SMEM(table.shape, jnp.float32),
            pltpu.VMEM((QUARTERS, pair_local, col_count), jnp.bfloat16),
            pltpu.VMEM((pair_local, now), jnp.bfloat16),
            pltpu.VMEM((width, now), jnp.float32),
            pltpu.SemaphoreType.DMA((QUARTERS,)),
            pltpu.SemaphoreType.DMA((2,)),
        ],
        compiler_params=pltpu.CompilerParams(vmem_limit_bytes=36 << 20),
    )(*held)
    return outs[:-1], outs[-1]


def last_stream(pairs, scaled, stream):
    pair_local, width = pairs.shape
    columns = scaled.shape[1]
    shapes = stream[0]

    part = pair_local // QUARTERS

    def body(pairs_ref, scaled_ref, *refs):
        pair_ref, turned_ref, sum_ref, rows_ref, done = refs[len(shapes) :]

        def fetch(step):
            return pltpu.make_async_copy(pairs_ref.at[step * part : step * part + part], pair_ref.at[step], done.at[step])

        for step in range(QUARTERS):
            fetch(step).start()
        turned_ref[...] = jnp.transpose(scaled_ref[...])
        for step in range(QUARTERS):
            fetch(step).wait()
            product = jnp.dot(
                turned_ref[:, step * part : step * part + part], pair_ref[step], preferred_element_type=jnp.float32
            )
            if step == 0:
                sum_ref[...] = product
            elif step < QUARTERS - 1:
                sum_ref[...] += product
            else:
                rows_ref[...] = jnp.transpose(sum_ref[...] + product)
        store([stream], refs, rows_ref)

    return pl.pallas_call(
        body,
        in_specs=[pl.BlockSpec(memory_space=pltpu.HBM), pl.BlockSpec(memory_space=pltpu.VMEM)],
        out_specs=[pl.BlockSpec(shape, lambda: (0, 0)) for shape in shapes],
        out_shape=[pltpu.HBM(shape, jnp.float32) for shape in shapes],
        scratch_shapes=[
            pltpu.VMEM((QUARTERS, part, width), jnp.bfloat16),
            pltpu.VMEM((columns, pair_local), jnp.bfloat16),
            pltpu.VMEM((columns, width), jnp.float32),
            pltpu.VMEM((width, columns), jnp.float32),
            pltpu.SemaphoreType.DMA((QUARTERS,)),
        ],
        compiler_params=pltpu.CompilerParams(vmem_limit_bytes=24 << 20),
    )(pltpu.with_memory_space_constraint(pairs, pltpu.HBM), scaled)


def local(pair_density_matrices, energy_bins, bin_weights, coulomb, state_matrices):
    width = pair_density_matrices.shape[1]
    pair_count = lax.axis_size("pair")
    sigma_count = lax.axis_size("sigma")
    row_count = width // pair_count
    col_count = width // sigma_count
    pair_position = lax.axis_index("pair")
    quarter = spots()[0]
    rc, n = row_count, COLUMNS
    slots = [(y, keeps, k) for y in range(NY) for keeps in (0, 1) for k in range(NZ)]

    def block(k):
        return slice(k * rc, k * rc + rc)

    b_stores = [(0, (y, block(keeps * NZ + k)), keeps, Z_ORDER[k], y) for y, keeps, k in slots]
    c_stores = [(keeps, (block(y * NZ + k),), keeps, Z_ORDER[k], -1 - y) for y, keeps, k in slots]
    a_shapes = [(NY * NX * rc // 2, n)] * 2
    a_shapes += [((high - low) * NY * NX * rc, n) for low, high in Z_SLICES[1:]]
    a_stores = []
    for y, keeps, k in slots:
        if k == 0:
            out, row = divmod(y * NX + keeps, NY * NX // 2)
        else:
            out, (low, _) = next((j, span) for j, span in enumerate(Z_SLICES) if span[0] <= k < span[1])
            out, row = out + 1, ((k - low) * NY + y) * NX + keeps
        a_stores.append((out, (block(row),), keeps, Z_ORDER[k], -1 - y))

    (b, *c), scaled = first_streams(
        pair_density_matrices,
        energy_bins.T,
        bin_weights,
        [([(NY, NX * NZ * rc, n)], b_stores), ([(NY * NZ * rc, n)] * 2, c_stores)],
    )
    a = last_stream(pair_density_matrices, scaled, (a_shapes, a_stores))

    c = x_added(c[1], x_swap(c[0]))
    c = y_direct(c)
    b = halves_added(y_parts(b))
    bc = interleaved(b[1], x_swap(b[0]), c, rc)
    bc = z_sum(*bc)
    a = y_direct(z_sum_both(*a))
    a = [(a[0][rows] + a[1][rows]) + (a[2][rows] + a[3][rows]) for rows in (slice(0, rc), slice(rc, None))]
    root = jnp.sqrt(coulomb)
    root_rows = -lax.dynamic_slice_in_dim(root, pair_position * row_count, row_count, 0)
    root_columns = lax.dynamic_slice_in_dim(root, quarter * col_count, col_count, 0)
    root_columns = jnp.concatenate([root_columns, root_columns])
    screened = screened_block(bc, a[1], x_swap(a[0]), root_rows[:, None], root_columns[None, :])
    screened = screened.reshape(row_count, -1, col_count)
    gathered = lax.all_gather(screened, "sigma")
    upper = quarter != lax.axis_index("sigma")
    parts = [jnp.where(upper, gathered[k ^ 2], gathered[k]) for k in range(sigma_count)]
    states_wide = state_matrices.astype(jnp.float32)
    applied = jnp.einsum(
        "rfc,cn->rfn", jnp.concatenate(parts, axis=2), states_wide, precision=lax.Precision.HIGHEST
    )
    own_states = lax.dynamic_slice_in_dim(states_wide, pair_position * row_count, row_count, 0)
    total = jnp.sum(own_states[:, None, :] * applied, axis=0) / jnp.float32(width)
    tile = total.reshape(8, -1)
    tile += lax.ppermute(tile, "pair", [(p, p ^ (NZ * NY)) for p in range(pair_count)])
    spread = jnp.broadcast_to(tile[None], (NZ * NY,) + tile.shape)
    total = jnp.sum(lax.all_to_all(spread, "pair", 0, 0, axis_index_groups=X_GROUPS, tiled=True), axis=0).reshape(total.shape)
    return (applied, total)


def solution(mesh):
    return jax.shard_map(
        local,
        mesh=mesh,
        in_specs=(P("pair", None), P("pair", None), P(), P(), P(None, "sigma")),
        out_specs=(P("pair", None, "sigma"), P(None, "sigma")),
        check_vma=False,
    )
```

```python
import jax
import jax.numpy as jnp
from jax import lax
from jax.experimental import pallas as pl
from jax.experimental.pallas import tpu as pltpu
from jax.sharding import PartitionSpec as P


NX, NZ, NY = 2, 8, 4
COLUMNS = 256
QUARTERS = 4
Z_ORDER = (4, 1, 3, -1, -3, 0, 2, -2)
Z_SLICES = ((0, 1), (1, 3), (3, 5), (5, 6), (6, 7), (7, 8))
X_GROUPS = [list(range(x * NZ * NY, (x + 1) * NZ * NY)) for x in range(NX)]


def place(position):
    return position // (NZ * NY), position // NY % NZ, position % NY


def z_perm(dz):
    moves = []
    for position in range(NX * NZ * NY):
        x, z, y = place(position)
        moves.append((position, (x * NZ + (z + dz) % NZ) * NY + y))
    return moves


def x_swap(away):
    pair_count, sigma_count = lax.axis_size("pair"), lax.axis_size("sigma")
    moves = [
        (p * sigma_count + s, (p ^ (NZ * NY)) * sigma_count + (s ^ 2))
        for p in range(pair_count)
        for s in range(sigma_count)
    ]
    return lax.ppermute(away, ("pair", "sigma"), moves)


def y_send(part, dy):
    moves = []
    for position in range(NX * NZ * NY):
        x, z, y = place(position)
        moves.append((position, (x * NZ + z) * NY + (y + dy) % NY))
    return lax.ppermute(part, "pair", moves)


def y_direct(blocks):
    return [blocks[-1]] + [y_send(blocks[dy - 1], dy) for dy in (1, 3, 2)]


def z_send(part, dz):
    return lax.ppermute(part, "pair", z_perm(dz))


def z_sum(far, up, down, keep, above, below):
    rows = keep.shape[0]
    far, up, down = z_send(far, -2), z_send(up, 1), z_send(down, -1)
    above = z_send(above + up[rows:], 2)
    below = z_send(below + down[rows:] + far, -2)
    return keep, up, down, above, below


def z_sum_both(low, high, up, down, keep, above, below):
    rows, columns = keep.shape
    half = rows // 2
    low, high = z_send(low, -2), z_send(high, 2)
    up, down = z_send(up, 1), z_send(down, -1)

    def middle(low, high, up, down, keep, above, below, above_out, below_out, keep_out):
        above_out[:half] = above[:half] + up[rows : rows + half]
        above_out[half:] = (above[half:] + up[rows + half :]) + high[...]
        below_out[:half] = (below[:half] + down[rows : rows + half]) + low[...]
        below_out[half:] = below[half:] + down[rows + half :]
        keep_out[...] = (keep[...] + up[:rows]) + down[:rows]

    keep, above, below = (pltpu.with_memory_space_constraint(part, pltpu.HBM) for part in (keep, above, below))
    above, below, keep = on_chip(middle, [(rows, columns)] * 3)(low, high, up, down, keep, above, below)
    above, below = z_send(above, 2), z_send(below, -2)

    part = rows // NY

    def last(above, below, keep, *outs):
        for k, out in enumerate(outs):
            span = slice(k * part, k * part + part)
            out[...] = keep[span] + (above[span] + below[span])

    return on_chip(last, [(part, columns)] * NY)(above, below, keep)


def on_chip(body, shapes):
    return pl.pallas_call(
        body,
        out_shape=[jax.ShapeDtypeStruct(shape, jnp.float32) for shape in shapes],
        compiler_params=pltpu.CompilerParams(vmem_limit_bytes=12 << 20),
    )


def halves_added(parts):
    half, columns = parts[0].shape[0] // 2, parts[0].shape[1]

    def body(one, two, three, four, *outs):
        for k, out in enumerate(outs):
            rows = slice(k * half, k * half + half)
            out[...] = (one[rows] + two[rows]) + (three[rows] + four[rows])

    return on_chip(body, [(half, columns)] * 2)(*parts)


def spots():
    position = lax.axis_index("pair")
    x = position // (NZ * NY)
    return lax.axis_index("sigma") ^ (2 * x), x, (position // NY) & (NZ - 1), position & (NY - 1)


def x_added(keep, other):
    rows = keep.shape[0] // NY

    def body(keep, other, *outs):
        for k, out in enumerate(outs):
            out[...] = keep[k * rows : k * rows + rows] + other[k * rows : k * rows + rows]

    return on_chip(body, [(rows, keep.shape[1])] * NY)(keep, other)


def interleaved(keep, other, two, row_count):
    columns = keep.shape[1]

    def body(keep, other, *refs):
        two, outs = refs[:NY], refs[NY:]
        for out, (low, high) in zip(outs, Z_SLICES):
            for k in range(low, high):
                rows = slice(k * row_count, k * row_count + row_count)
                at = 2 * (k - low) * row_count
                out[at : at + row_count] = keep[rows] + other[rows]
                out[at + row_count : at + 2 * row_count] = (two[0][rows] + two[1][rows]) + (two[2][rows] + two[3][rows])

    return on_chip(body, [(2 * (high - low) * row_count, columns) for low, high in Z_SLICES])(keep, other, *two)


def screened_block(ring, keep, other, root_rows, root_columns):
    rows, columns = keep.shape

    def body(kept, up, down, above, below, keep, other, by_row, by_column, out):
        for k in range(2):
            part = slice(k * rows, k * rows + rows)
            total = ((kept[part] + up[part]) + down[part]) + (above[part] + below[part])
            span = slice(k * columns, k * columns + columns)
            out[:, span] = by_row[...] * total * by_column[:, span]
        out[:, 2 * columns :] = by_row[...] * (keep[...] + other[...]) * by_column[:, 2 * columns :]

    return on_chip(body, [(rows, 3 * columns)])(*ring, keep, other, root_rows, root_columns)[0]


def fetcher(pairs_ref, pair_ref, done):
    col_count = pair_ref.shape[2]
    quarter = spots()[0]

    def first_column(step):
        return pl.multiple_of(((quarter + step) & (QUARTERS - 1)) * col_count, 128)

    def fetch(step):
        part = pairs_ref.at[:, pl.ds(first_column(step), col_count)]
        return pltpu.make_async_copy(part, pair_ref.at[step], done.at[step])

    return first_column, fetch


def multiply(first_column, fetch, pair_ref, scaled_ref, rows_ref, waited):
    for step in range(QUARTERS):
        if step >= waited:
            fetch(step).wait()
        rows_ref[pl.ds(first_column(step), pair_ref.shape[2]), :] = lax.dot_general(
            pair_ref[step],
            scaled_ref[:, : rows_ref.shape[1]],
            (((0,), (0,)), ((), ())),
            preferred_element_type=jnp.float32,
        )


def store(streams, outs, rows_ref):
    _, x, z, own_y = spots()
    before = 0
    for k, (stream, stores) in enumerate(streams):
        for out, index, keeps, dz, y in stores:
            y = y if y >= 0 else (own_y - y) & (NY - 1)
            at = ((x if keeps else 1 - x) * NZ + ((z + dz) & (NZ - 1))) * NY + y
            row_count = rows_ref.shape[0] // (NX * NZ * NY)
            rows = pl.ds(pl.multiple_of(at * row_count, 8), row_count)
            outs[before + out][index] = rows_ref[rows, k * COLUMNS : k * COLUMNS + COLUMNS]
        before += len(stream)


def first_streams(pairs, bins, table, streams):
    pair_local, width = pairs.shape
    col_count = width // QUARTERS
    total = 2 * col_count
    now = COLUMNS * len(streams)
    shapes = [shape for stream, _ in streams for shape in stream]
    count = len(shapes)

    def body(pairs_ref, bins_hbm, table_hbm, *refs):
        later_ref, bins_ref, table_ref, pair_ref, scaled_ref, rows_ref, done, small = refs[count:]
        first_column, fetch = fetcher(pairs_ref, pair_ref, done)
        bins_copy = pltpu.make_async_copy(bins_hbm, bins_ref, small.at[0])
        table_copy = pltpu.make_async_copy(table_hbm, table_ref, small.at[1])
        bins_copy.start()
        table_copy.start()
        for step in range(QUARTERS):
            fetch(step).start()
        bins_copy.wait()
        table_copy.wait()
        index = bins_ref[...]
        upper = lax.broadcasted_iota(jnp.int32, index.shape, 0) > 0
        picked = jnp.zeros(index.shape, jnp.float32)
        for level in range(table.shape[1]):
            picked = jnp.where(index == level, jnp.where(upper, table_ref[1, level], table_ref[0, level]), picked)
        weight = picked / jnp.float32(pair_local * NX * NZ * NY)
        by_pair = jnp.transpose(jnp.concatenate([weight, jnp.zeros((6, pair_local), jnp.float32)], axis=0))
        fetch(0).wait()

        def scaled(t):
            f, column = divmod(128 * t, col_count)
            product = by_pair[:, f : f + 1] * pair_ref[0, :, column : column + 128].astype(jnp.float32)
            return product.astype(jnp.bfloat16)

        for t in range(now // 128):
            scaled_ref[:, 128 * t : 128 * t + 128] = scaled(t)
        multiply(first_column, fetch, pair_ref, scaled_ref, rows_ref, 1)
        for t in range(now // 128, total // 128):
            later_ref[:, 128 * t - now : 128 * t - now + 128] = scaled(t)
        store(streams, refs, rows_ref)

    held = [pltpu.with_memory_space_constraint(array, pltpu.HBM) for array in (pairs, bins, table)]
    outs = pl.pallas_call(
        body,
        in_specs=[pl.BlockSpec(memory_space=pltpu.HBM)] * 3,
        out_specs=[pl.BlockSpec(memory_space=pltpu.VMEM)] * (count + 1),
        out_shape=[jax.ShapeDtypeStruct(shape, jnp.float32) for shape in shapes]
        + [jax.ShapeDtypeStruct((pair_local, total - now), jnp.bfloat16)],
        scratch_shapes=[
            pltpu.VMEM(bins.shape, jnp.int32),
            pltpu.SMEM(table.shape, jnp.float32),
            pltpu.VMEM((QUARTERS, pair_local, col_count), jnp.bfloat16),
            pltpu.VMEM((pair_local, now), jnp.bfloat16),
            pltpu.VMEM((width, now), jnp.float32),
            pltpu.SemaphoreType.DMA((QUARTERS,)),
            pltpu.SemaphoreType.DMA((2,)),
        ],
        compiler_params=pltpu.CompilerParams(vmem_limit_bytes=36 << 20),
    )(*held)
    return outs[:-1], outs[-1]


def last_stream(pairs, scaled, stream):
    pair_local, width = pairs.shape
    columns = scaled.shape[1]
    shapes = stream[0]

    part = pair_local // QUARTERS

    def body(pairs_ref, scaled_ref, *refs):
        pair_ref, turned_ref, sum_ref, rows_ref, done = refs[len(shapes) :]

        def fetch(step):
            return pltpu.make_async_copy(pairs_ref.at[step * part : step * part + part], pair_ref.at[step], done.at[step])

        for step in range(QUARTERS):
            fetch(step).start()
        turned_ref[...] = jnp.transpose(scaled_ref[...])
        for step in range(QUARTERS):
            fetch(step).wait()
            product = jnp.dot(
                turned_ref[:, step * part : step * part + part], pair_ref[step], preferred_element_type=jnp.float32
            )
            if step == 0:
                sum_ref[...] = product
            elif step < QUARTERS - 1:
                sum_ref[...] += product
            else:
                rows_ref[...] = jnp.transpose(sum_ref[...] + product)
        store([stream], refs, rows_ref)

    return pl.pallas_call(
        body,
        in_specs=[pl.BlockSpec(memory_space=pltpu.HBM), pl.BlockSpec(memory_space=pltpu.VMEM)],
        out_specs=[pl.BlockSpec(shape, lambda: (0, 0)) for shape in shapes],
        out_shape=[pltpu.HBM(shape, jnp.float32) for shape in shapes],
        scratch_shapes=[
            pltpu.VMEM((QUARTERS, part, width), jnp.bfloat16),
            pltpu.VMEM((columns, pair_local), jnp.bfloat16),
            pltpu.VMEM((columns, width), jnp.float32),
            pltpu.VMEM((width, columns), jnp.float32),
            pltpu.SemaphoreType.DMA((QUARTERS,)),
        ],
        compiler_params=pltpu.CompilerParams(vmem_limit_bytes=24 << 20),
    )(pltpu.with_memory_space_constraint(pairs, pltpu.HBM), scaled)


def local(pair_density_matrices, energy_bins, bin_weights, coulomb, state_matrices):
    width = pair_density_matrices.shape[1]
    pair_count = lax.axis_size("pair")
    sigma_count = lax.axis_size("sigma")
    row_count = width // pair_count
    col_count = width // sigma_count
    pair_position = lax.axis_index("pair")
    quarter = spots()[0]
    rc, n = row_count, COLUMNS
    slots = [(y, keeps, k) for y in range(NY) for keeps in (0, 1) for k in range(NZ)]

    def block(k):
        return slice(k * rc, k * rc + rc)

    b_stores = [(y, (block(keeps * NZ + k),), keeps, Z_ORDER[k], -1 - y) for y, keeps, k in slots]
    c_stores = [(keeps, (block(y * NZ + k),), keeps, Z_ORDER[k], -1 - y) for y, keeps, k in slots]
    a_shapes = [(NY * NX * rc // 2, n)] * 2
    a_shapes += [((high - low) * NY * NX * rc, n) for low, high in Z_SLICES[1:]]
    a_stores = []
    for y, keeps, k in slots:
        if k == 0:
            out, row = divmod(y * NX + keeps, NY * NX // 2)
        else:
            out, (low, _) = next((j, span) for j, span in enumerate(Z_SLICES) if span[0] <= k < span[1])
            out, row = out + 1, ((k - low) * NY + y) * NX + keeps
        a_stores.append((out, (block(row),), keeps, Z_ORDER[k], -1 - y))

    (*b, c_away, c_keep), scaled = first_streams(
        pair_density_matrices,
        energy_bins.T,
        bin_weights,
        [([(NX * NZ * rc, n)] * NY, b_stores), ([(NY * NZ * rc, n)] * 2, c_stores)],
    )
    a = last_stream(pair_density_matrices, scaled, (a_shapes, a_stores))

    c = x_added(c_keep, x_swap(c_away))
    c = y_direct(c)
    b = halves_added(y_direct(b))
    bc = interleaved(b[1], x_swap(b[0]), c, rc)
    bc = z_sum(*bc)
    a = y_direct(z_sum_both(*a))
    a = [(a[0][rows] + a[1][rows]) + (a[2][rows] + a[3][rows]) for rows in (slice(0, rc), slice(rc, None))]
    root = jnp.sqrt(coulomb)
    root_rows = -lax.dynamic_slice_in_dim(root, pair_position * row_count, row_count, 0)
    root_columns = lax.dynamic_slice_in_dim(root, quarter * col_count, col_count, 0)
    root_columns = jnp.concatenate([root_columns, root_columns])
    screened = screened_block(bc, a[1], x_swap(a[0]), root_rows[:, None], root_columns[None, :])
    screened = screened.reshape(row_count, -1, col_count)
    gathered = lax.all_gather(screened, "sigma")
    upper = quarter != lax.axis_index("sigma")
    parts = [jnp.where(upper, gathered[k ^ 2], gathered[k]) for k in range(sigma_count)]
    states_wide = state_matrices.astype(jnp.float32)
    applied = jnp.einsum(
        "rfc,cn->rfn", jnp.concatenate(parts, axis=2), states_wide, precision=lax.Precision.HIGHEST
    )
    own_states = lax.dynamic_slice_in_dim(states_wide, pair_position * row_count, row_count, 0)
    total = jnp.sum(own_states[:, None, :] * applied, axis=0) / jnp.float32(width)
    tile = total.reshape(8, -1)
    tile += lax.ppermute(tile, "pair", [(p, p ^ (NZ * NY)) for p in range(pair_count)])
    spread = jnp.broadcast_to(tile[None], (NZ * NY,) + tile.shape)
    total = jnp.sum(lax.all_to_all(spread, "pair", 0, 0, axis_index_groups=X_GROUPS, tiled=True), axis=0).reshape(total.shape)
    return (applied, total)


def solution(mesh):
    return jax.shard_map(
        local,
        mesh=mesh,
        in_specs=(P("pair", None), P("pair", None), P(), P(), P(None, "sigma")),
        out_specs=(P("pair", None, "sigma"), P(None, "sigma")),
        check_vma=False,
    )
```
